32 devices in a mesh: batch: 4 (over y, x), corpus: 8 (over z, core).
Axes of the slice: x: 2, y: 2, z: 4, core: 2. Of those that a mesh axis runs over, the one named last changes fastest.
Arguments:
- states: bfloat16 [4096, 4096], P('batch', 'corpus'), may hold values from -6 to 6
- norm_gain: float32 [4096], replicated, may hold values from 0.25 to 1.75
- gate_weight: bfloat16 [4096, 12288], P('batch', 'corpus'), may hold values from -0.09375 to 0.09375
- up_weight: bfloat16 [4096, 12288], P('batch', 'corpus'), may hold values from -0.09375 to 0.09375
- down_weight: bfloat16 [12288, 4096], P('corpus', 'batch'), may hold values from -0.0546875 to 0.0546875
- final_gain: float32 [4096], replicated, may hold values from 0.25 to 1.75
- hash_weight: bfloat16 [4096, 1024], replicated, may hold values from -0.75 to 0.75
- query_bits: bfloat16 [4096, 1024], replicated, may hold values from -1 to 1
- slot_map: int32 [64], replicated, may hold values from 0 to 63, each once
- query_index: int32 [4096, 100], replicated, may hold values from 0 to 63
Outputs:
- scores: float32 [4096, 100], P(('batch', 'corpus'))
The draws below stay inside these ranges and needn't reach their ends.
Inputs may be any that keep to these rules, and one draw needn't show every extreme that they name: `slot_map`: each corpus entry is named by exactly one document.
All inputs are finite; a program needn't handle non-finite values.
Results may differ from the reference program's by a relative error of at most 0.017.
Values may be sent and summed in bfloat16 or wider, within the bound.
A program may use at most 192 MiB of HBM per device.

```python
import jax
import jax.numpy as jnp
from jax import lax

D = 4096
FF = 12288
DOC_LEN = 64
CODE = 1024
NQ = 4096
TOPK = 100
NDOC = 64
TOKENS = 4096
N_CORPUS = 8


def draw_query_bits(key, part):
    picks = jax.random.randint(jax.random.fold_in(key, 7), (NQ, CODE), 0, 2)
    return (2.0 * picks.astype(jnp.float32) - 1.0).astype(jnp.bfloat16)


def plant(entries, stream_key, low, high):
    longest = entries.shape.index(max(entries.shape))
    spots = []
    for shift in (0, 1):
        where = [jax.random.randint(jax.random.fold_in(stream_key, axis), (), 0, length) for axis, length in enumerate(entries.shape)]
        where[longest] = (where[longest] + shift) % entries.shape[longest]
        spots.append(tuple(where))
    return entries.at[spots[0]].set(low).at[spots[1]].set(high)


def steps_of(own_key, shape, cuts, low, largest):
    def one(position, shards_of):
        heights = jax.random.uniform(jax.random.fold_in(jax.random.fold_in(own_key, 6), position), (shards_of,), jnp.float32, low / len(cuts), largest / len(cuts))
        return jnp.repeat(jnp.exp(heights), shape[position] // shards_of).reshape((-1,) + (1,) * (len(shape) - position - 1))

    level = one(*cuts[0])
    for cut in cuts[1:]:
        level = level * one(*cut)
    return level


def scatter_about(stream_key, dims, scale, reach, pieces=(), dtype=jnp.bfloat16):
    result = jax.random.normal(stream_key, dims, jnp.float32) * scale
    if len(pieces) > 0:
        result = steps_of(stream_key, dims, pieces, -0.22, 0.18) * result
    return jnp.clip(result, min=-reach, max=reach).astype(dtype)


def setup_inputs(seed: int = 0) -> dict:
    key_list = jax.random.split(jax.random.key(seed), 11)
    return {
        "states": scatter_about(key_list[0], (TOKENS, D), 1.0, 6.0, ((0, 4), (1, 8))),
        "norm_gain": jnp.clip(1.0 + 0.15 * jax.random.normal(key_list[1], (D,), jnp.float32), 0.25, 1.75),
        "gate_weight": scatter_about(key_list[2], (D, FF), D ** -0.5, 0.09375, ((0, 4), (1, 8))),
        "up_weight": scatter_about(key_list[3], (D, FF), D ** -0.5, 0.09375, ((0, 4), (1, 8))),
        "down_weight": scatter_about(key_list[4], (FF, D), FF ** -0.5, 0.0546875, ((0, 8), (1, 4))),
        "final_gain": jnp.clip(1.0 + 0.15 * jax.random.normal(key_list[5], (D,), jnp.float32), 0.25, 1.75),
        "hash_weight": scatter_about(key_list[6], (D, CODE), (D // 64) ** -0.5, 0.75),
        "query_bits": draw_query_bits(jax.random.fold_in(key_list[10], 71), 0),
        "slot_map": jax.random.permutation(key_list[8], NDOC).astype(jnp.int32),
        "query_index": plant(jax.random.randint(key_list[9], (NQ, TOPK), 0, NDOC), jax.random.fold_in(key_list[9], 1), 0, NDOC - 1).astype(jnp.int32),
    }


def rms(values, gain):
    return values * lax.rsqrt(lax.optimization_barrier(jnp.mean(values * values, axis=-1, keepdims=True)) + 1e-06) * gain

def reference(states, norm_gain, gate_weight, up_weight, down_weight, final_gain, hash_weight, query_bits, slot_map, query_index):
    floats = states.astype(jnp.float32)
    normed = rms(floats, norm_gain).astype(jnp.bfloat16)
    gate = jnp.dot(normed, gate_weight, preferred_element_type=jnp.float32)
    up = jnp.dot(normed, up_weight, preferred_element_type=jnp.float32)
    hidden = (jax.nn.silu(gate) * up).astype(jnp.bfloat16)
    width = FF // N_CORPUS
    hidden_groups = hidden.reshape(TOKENS, N_CORPUS, width).transpose(1, 0, 2)
    down_groups = down_weight.reshape(N_CORPUS, width, D)

    def add_group(total, pair):
        part = jnp.dot(pair[0], pair[1], preferred_element_type=jnp.float32).astype(jnp.bfloat16)
        return (total + part.astype(jnp.float32), None)
    ffn, unused = lax.scan(add_group, jnp.zeros((TOKENS, D), jnp.float32), (hidden_groups, down_groups))
    resid = floats + ffn
    finals = rms(resid, final_gain)
    pooled = lax.optimization_barrier(jnp.mean(finals.reshape(NDOC, DOC_LEN, D), axis=1)).astype(jnp.bfloat16)
    codes = jnp.tanh(jnp.dot(pooled, hash_weight, preferred_element_type=jnp.float32)).astype(jnp.bfloat16)
    corpus = jnp.zeros((NDOC, CODE), jnp.bfloat16).at[slot_map].set(codes)
    table = jnp.dot(query_bits, corpus.T, preferred_element_type=jnp.float32) / jnp.sqrt(jnp.float32(CODE))
    return jnp.take_along_axis(table, query_index, axis=1)
```

```python
import jax
import jax.numpy as jnp
from jax import lax
from jax.experimental import pallas as pl
from jax.experimental.pallas import tpu as pltpu
from jax.sharding import PartitionSpec as P

DOC_LEN = 64
CODE = 1024
NQ = 4096


def rms(values, gain):
    return values * lax.rsqrt(jnp.mean(values * values, axis=-1, keepdims=True) + 1e-06) * gain


def add_rows(left, piece):
    return jnp.dot(left, piece, preferred_element_type=jnp.float32)


def score_kernel(bits_ref, corpus_ref, index_ref, out_ref):
    table = lax.dot_general(
        bits_ref[...],
        corpus_ref[...],
        (((1,), (1,)), ((), ())),
        preferred_element_type=jnp.float32,
    ) * (1.0 / float(bits_ref.shape[1]) ** 0.5)
    out_ref[...] = jnp.take_along_axis(table, index_ref[...], axis=1)


def score(bits, corpus, index):
    rows, top = index.shape
    lanes = 128 * max(pl.cdiv(corpus.shape[0], 128), pl.cdiv(top, 128))
    corpus = jnp.pad(corpus, ((0, lanes - corpus.shape[0]), (0, 0)))
    index = jnp.pad(index, ((0, 0), (0, lanes - top)))
    wide = pl.pallas_call(
        score_kernel, out_shape=jax.ShapeDtypeStruct((rows, lanes), jnp.float32)
    )(bits, corpus, index)
    return wide[:, :top]


def local(
    states,
    norm_gain,
    gate_weight,
    up_weight,
    down_weight,
    final_gain,
    hash_weight,
    query_bits,
    slot_map,
    query_index,
):
    corpus_count = lax.axis_size("corpus")
    devices = lax.axis_size("batch") * corpus_count
    flat_index = lax.axis_index("batch") * corpus_count + lax.axis_index("corpus")
    whole = lax.all_gather(states, "corpus", axis=1, tiled=True)
    normed = rms(whole.astype(jnp.float32), norm_gain).astype(jnp.bfloat16)

    def add_one(piece):
        return add_rows(normed, piece)

    gate = add_one(lax.all_gather(gate_weight, "batch", axis=0, tiled=True))
    up = add_one(lax.all_gather(up_weight, "batch", axis=0, tiled=True))
    hidden = (jax.nn.silu(gate) * up).astype(jnp.bfloat16)
    terms = jnp.dot(
        hidden,
        lax.all_gather(down_weight, "batch", axis=1, tiled=True),
        preferred_element_type=jnp.float32,
    )
    ffn = lax.psum_scatter(
        terms.astype(jnp.bfloat16), "corpus", scatter_dimension=0, tiled=True
    ).astype(jnp.float32)
    own_rows = ffn.shape[0]
    mine = lax.dynamic_slice_in_dim(whole, lax.axis_index("corpus") * own_rows, own_rows, 0)
    resid = mine.astype(jnp.float32) + ffn
    finals = rms(resid, final_gain)
    owned_docs = own_rows // DOC_LEN
    pooled = jnp.mean(finals.reshape(owned_docs, DOC_LEN, finals.shape[1]), axis=1).astype(
        jnp.bfloat16
    )
    codes = jnp.tanh(jnp.dot(pooled, hash_weight, preferred_element_type=jnp.float32)).astype(
        jnp.bfloat16
    )
    doc_total = owned_docs * devices
    gathered = lax.all_gather(codes, ("batch", "corpus"), axis=0, tiled=True)
    placing = (slot_map[:, None] == jnp.arange(doc_total, dtype=jnp.int32)[None, :]).astype(
        jnp.bfloat16
    )
    corpus = jnp.einsum("ds,dc->sc", placing, gathered, preferred_element_type=jnp.float32).astype(
        jnp.bfloat16
    )
    query_rows = NQ // devices
    my_bits = lax.dynamic_slice_in_dim(query_bits, flat_index * query_rows, query_rows, 0)
    my_index = lax.dynamic_slice_in_dim(query_index, flat_index * query_rows, query_rows, 0)
    return score(my_bits, corpus, my_index)


def solution(mesh):
    placed = (
        P("batch", "corpus"),
        P(),
        P("batch", "corpus"),
        P("batch", "corpus"),
        P("corpus", "batch"),
        P(),
        P(),
        P(),
        P(),
        P(),
    )
    return jax.shard_map(
        local, mesh=mesh, in_specs=placed, out_specs=P(("batch", "corpus"), None), check_vma=False
    )
```

```python
import jax
import jax.numpy as jnp
from jax import lax
from jax.experimental import pallas as pl
from jax.experimental.pallas import tpu as pltpu
from jax.sharding import PartitionSpec as P

DOC_LEN = 64
CODE = 1024
NQ = 4096


def rms(values, gain):
    return values * lax.rsqrt(jnp.mean(values * values, axis=-1, keepdims=True) + 1e-06) * gain


def add_rows(left, piece):
    return jnp.dot(left, piece, preferred_element_type=jnp.float32)


def score_kernel(bits_ref, corpus_ref, index_ref, out_ref):
    table = lax.dot_general(
        bits_ref[...],
        corpus_ref[...],
        (((1,), (1,)), ((), ())),
        preferred_element_type=jnp.float32,
    ) * (1.0 / float(bits_ref.shape[1]) ** 0.5)
    out_ref[...] = jnp.take_along_axis(table, index_ref[...], axis=1)


def score(bits, corpus, index):
    rows, top = index.shape
    lanes = 128 * max(pl.cdiv(corpus.shape[0], 128), pl.cdiv(top, 128))
    corpus = jnp.pad(corpus, ((0, lanes - corpus.shape[0]), (0, 0)))
    index = jnp.pad(index, ((0, 0), (0, lanes - top)))
    wide = pl.pallas_call(
        score_kernel, out_shape=jax.ShapeDtypeStruct((rows, lanes), jnp.float32)
    )(bits, corpus, index)
    return wide[:, :top]


def wide_kernel(
    states_ref, gain_ref, gate_ref, up_ref, down_ref, out_ref,
    X, G, U, W, N, H, SR, YR, ZR,
    s_loc, s_y, s_zr, s_zl, s_sib, w_loc, w_x, w_y, w_r, c_sib, c_y, c_z,
):
    nz = lax.axis_size("corpus") // 2
    b = lax.axis_index("batch")
    c = lax.axis_index("corpus")
    y, x = b // 2, b % 2
    z, k = c // 2, c % 2
    rows, feat = states_ref.shape
    half = W.shape[0]
    full = X.shape[1]
    cols = down_ref.shape[1]
    w = cols // 2
    by, bx, bd = (1 - y) * 2 + x, y * 2 + (1 - x), (1 - y) * 2 + (1 - x)
    to_y = {"batch": by}
    to_x = {"batch": bx}
    to_sib = {"corpus": z * 2 + (1 - k)}

    def at_z(other):
        return {"corpus": other * 2 + k}

    def remote(src, dst, sems, place):
        return pltpu.make_async_remote_copy(
            src_ref=src, dst_ref=dst, send_sem=sems.at[0], recv_sem=sems.at[1],
            device_id=place, device_id_type=pl.DeviceIdType.MESH,
        )

    def spot(t, zs, ks):
        block = y if t == 0 else 1 - y
        return X.at[
            pl.ds(pl.multiple_of(block * rows, rows), rows),
            pl.ds(pl.multiple_of((zs * 2 + ks) * feat, feat), feat),
        ]

    own_states = pltpu.make_async_copy(states_ref, spot(0, z, k), s_loc)
    y_states = remote(states_ref, X.at[
        pl.ds(pl.multiple_of(y * rows, rows), rows),
        pl.ds(pl.multiple_of(c * feat, feat), feat),
    ], s_y, to_y)

    def right(t, s):
        src = states_ref if t == 0 and s == 0 else spot(t, z - s, k)
        return remote(src, spot(t, z - s, k), s_zr.at[t, s], at_z(z + 1))

    def left(t, s):
        src = states_ref if t == 0 and s == 0 else spot(t, z + s, k)
        return remote(src, spot(t, z + s, k), s_zl.at[t, s], at_z(z - 1))

    def sib(t, zs):
        return remote(spot(t, zs, k), spot(t, zs, k), s_sib.at[t, zs], to_sib)

    def sib_in(t, zs):
        return remote(spot(t, zs, 1 - k), spot(t, zs, 1 - k), s_sib.at[t, zs], to_sib)

    def first(t):
        @pl.when(z + 1 < nz)
        def _():
            right(t, 0).start()

        @pl.when(z >= 1)
        def _():
            left(t, 0).start()

        sib(t, z).start()

    def relay(t, s):
        @pl.when(z - 1 - s >= 0)
        def _():
            right(t, s).wait_recv()
            if s + 1 < nz - 1:
                @pl.when(z + 1 < nz)
                def _():
                    right(t, s + 1).start()
            sib(t, z - 1 - s).start()

        @pl.when(z + 1 + s < nz)
        def _():
            left(t, s).wait_recv()
            if s + 1 < nz - 1:
                @pl.when(z >= 1)
                def _():
                    left(t, s + 1).start()
            sib(t, z + 1 + s).start()

    def part(m, mine):
        h = pl.ds(pl.multiple_of((y if mine else 1 - y) * half, half), half)
        if m == 2:
            return down_ref.at[h, :]
        return (gate_ref, up_ref)[m].at[:, h]

    def place(m, block):
        if m == 2:
            return W.at[:, pl.ds(pl.multiple_of(block * cols, cols), cols)]
        return (G, U)[m].at[pl.ds(pl.multiple_of(block * rows_w, rows_w), rows_w), :]

    rows_w = gate_ref.shape[0]
    loc = [pltpu.make_async_copy(part(m, True), place(m, b), w_loc.at[m]) for m in range(3)]
    wx = [remote(part(m, True), place(m, b), w_x.at[m], to_x) for m in range(3)]
    wy = [remote(part(m, False), place(m, b), w_y.at[m], to_y) for m in range(3)]
    wr = [remote(place(m, by), place(m, by), w_r.at[m], to_x) for m in range(3)]

    y_states.start()
    own_states.start()
    wx[0].start()
    for m in range(3):
        wy[m].start()
    wx[1].start()
    own_states.wait()
    first(0)
    for m in range(3):
        loc[m].start()
    y_states.wait_recv()
    first(1)
    for s in range(nz - 1):
        relay(0, s)
        if s == nz - 2:
            wy[0].wait_recv()
            wr[0].start()
    for s in range(nz - 1):
        relay(1, s)
        if s == 0:
            wy[1].wait_recv()
            wr[1].start()
            wx[2].start()
    wy[2].wait_recv()
    wr[2].start()
    for m in range(3):
        loc[m].wait()
    for t in range(2):
        for zs in range(nz):
            sib_in(t, zs).wait_recv()
    for m in range(2):
        wx[m].wait_recv()
        wr[m].wait_recv()
    y_states.wait_send()
    for t in range(2):
        for zs in range(nz):
            sib(t, zs).wait_send()
        for s in range(nz - 1):
            @pl.when((z - s >= 0) & (z + 1 < nz))
            def _():
                right(t, s).wait_send()

            @pl.when((z + s < nz) & (z >= 1))
            def _():
                left(t, s).wait_send()

    tile = N.shape[0]
    gain = gain_ref[...]

    @pl.loop(0, X.shape[0] // tile)
    def _(i):
        r = pl.ds(pl.multiple_of(i * tile, tile), tile)

        @pl.loop(0, tile // 32)
        def _(p):
            q = pl.multiple_of(p * 32, 32)
            v = X[pl.ds(pl.multiple_of(i * tile + q, 32), 32), :].astype(jnp.float32)
            scale = lax.rsqrt(jnp.mean(v * v, axis=-1, keepdims=True) + 1e-06)
            N[pl.ds(q, 32), :] = (v * scale * gain).astype(jnp.bfloat16)

        step = half // 3 if (half // 3) % 128 == 0 else 128

        @pl.loop(0, half // step)
        def _(j):
            h = pl.ds(pl.multiple_of(j * step, 128), step)
            g = jnp.dot(N[...], G[:, h], preferred_element_type=jnp.float32)
            u = jnp.dot(N[...], U[:, h], preferred_element_type=jnp.float32)
            H[r, h] = (g * jax.nn.sigmoid(g) * u).astype(jnp.bfloat16)

    blocks = [x, 2 + x, 1 - x, 2 + (1 - x)]
    own_rows = out_ref.shape[0]
    for j in range(4):
        out_ref[:, pl.ds(pl.multiple_of(blocks[j] * w, w), w)] = X[
            pl.ds(pl.multiple_of(y * rows + z * own_rows, own_rows), own_rows),
            pl.ds(pl.multiple_of(blocks[j] * cols + k * w, w), w),
        ].astype(jnp.float32)

    base = full // 2

    def down_cols(j, core):
        return pl.ds(pl.multiple_of(blocks[j] * cols + core * w, w), w)

    def sib_sum(j):
        return remote(X.at[:, pl.ds(j * w, w)], SR.at[j], c_sib.at[j], to_sib)

    def y_sum(j):
        return remote(X.at[pl.ds(0, rows), pl.ds(base + j * w, w)], YR.at[j], c_y.at[j], to_y)

    def z_sum(j, dz):
        to = lax.rem(z + dz, nz)
        return remote(
            X.at[
                pl.ds(pl.multiple_of(rows + to * own_rows, own_rows), own_rows),
                pl.ds(base + j * w, w),
            ],
            ZR.at[j, dz - 1], c_z.at[j, dz - 1], at_z(to),
        )

    piece = min(512, rows)

    def step_a(j):
        @pl.loop(0, 2 * rows // piece)
        def _(i):
            r = pl.ds(pl.multiple_of(i * piece, piece), piece)
            X[r, pl.ds(j * w, w)] = jnp.dot(
                H[r, :], W[:, down_cols(j, 1 - k)], preferred_element_type=jnp.float32
            ).astype(jnp.bfloat16)

        sib_sum(j).start()

    def step_b(j):
        sib_sum(j).wait_recv()
        for put, block in ((0, 1 - y), (1, y)):
            @pl.loop(0, rows // piece)
            def _(i):
                r = pl.ds(pl.multiple_of(block * rows + i * piece, piece), piece)
                X[pl.ds(pl.multiple_of(put * rows + i * piece, piece), piece), pl.ds(base + j * w, w)] = (
                    jnp.dot(H[r, :], W[:, down_cols(j, k)], preferred_element_type=jnp.float32)
                    + SR[j, r, :].astype(jnp.float32)
                ).astype(jnp.bfloat16)

            if put == 0:
                y_sum(j).start()

    def step_c(j):
        y_sum(j).wait_recv()

        @pl.loop(0, rows // own_rows)
        def _(i):
            r = pl.ds(pl.multiple_of(rows + i * own_rows, own_rows), own_rows)
            here = pl.ds(base + j * w, w)
            X[r, here] = (
                X[r, here].astype(jnp.float32)
                + YR[j, pl.ds(pl.multiple_of(i * own_rows, own_rows), own_rows), :].astype(jnp.float32)
            ).astype(jnp.bfloat16)

        for dz in range(1, nz):
            z_sum(j, dz).start()

    def step_e(j):
        here = pl.ds(pl.multiple_of(blocks[j] * w, w), w)
        total = out_ref[:, here] + X[
            pl.ds(pl.multiple_of(rows + z * own_rows, own_rows), own_rows), pl.ds(base + j * w, w)
        ].astype(jnp.float32)
        for dz in range(1, nz):
            z_sum(j, dz).wait_recv()
            total = total + ZR[j, dz - 1].astype(jnp.float32)
        out_ref[:, here] = total

    step_a(0)
    step_a(1)
    step_b(0)
    step_b(1)
    wx[2].wait_recv()
    wr[2].wait_recv()
    step_a(2)
    step_c(0)
    step_a(3)
    step_b(2)
    step_c(1)
    step_b(3)
    step_e(0)
    step_c(2)
    step_e(1)
    step_c(3)
    step_e(2)
    step_e(3)
    for j in range(4):
        sib_sum(j).wait_send()
        y_sum(j).wait_send()
        for dz in range(1, nz):
            z_sum(j, dz).wait_send()
    for m in range(3):
        wx[m].wait_send()
        wy[m].wait_send()
        wr[m].wait_send()


def wide(states, norm_gain, gate_weight, up_weight, down_weight):
    nz = lax.axis_size("corpus") // 2
    rows, feat = states.shape
    full = norm_gain.shape[0]
    half = gate_weight.shape[1] // 2
    cols = down_weight.shape[1]
    w = cols // 2
    own_rows = rows // nz
    dma = pltpu.SemaphoreType.DMA
    tile = min(512, rows)
    any_spec = pl.BlockSpec(memory_space=pl.ANY)
    vmem = pl.BlockSpec(memory_space=pltpu.VMEM)
    return pl.pallas_call(
        wide_kernel,
        out_shape=jax.ShapeDtypeStruct((own_rows, full // 2), jnp.float32),
        in_specs=[any_spec, vmem, any_spec, any_spec, any_spec],
        out_specs=vmem,
        scratch_shapes=[
            pltpu.VMEM((2 * rows, full), jnp.bfloat16),
            pltpu.VMEM((full, half), jnp.bfloat16),
            pltpu.VMEM((full, half), jnp.bfloat16),
            pltpu.VMEM((half, full), jnp.bfloat16),
            pltpu.VMEM((tile, full), jnp.bfloat16),
            pltpu.VMEM((2 * rows, half), jnp.bfloat16),
            pltpu.VMEM((4, 2 * rows, w), jnp.bfloat16),
            pltpu.VMEM((4, rows, w), jnp.bfloat16),
            pltpu.VMEM((4, nz - 1, own_rows, w), jnp.bfloat16),
            dma, dma((2,)), dma((2, nz - 1, 2)), dma((2, nz - 1, 2)), dma((2, nz, 2)),
            dma((3,)), dma((3, 2)), dma((3, 2)), dma((3, 2)),
            dma((4, 2)), dma((4, 2)), dma((4, nz - 1, 2)),
        ],
        compiler_params=pltpu.CompilerParams(
            has_side_effects=True, vmem_limit_bytes=67043328
        ),
    )(states, norm_gain[None], gate_weight, up_weight, down_weight)


def code_kernel(resid_ref, gain_ref, hash_ref, out_ref, HV, SQ, PB, CA, h_sem, q_sem, p_sem, a_send, a_recv):
    corpus = lax.axis_size("corpus")
    devices = lax.axis_size("batch") * corpus
    b = lax.axis_index("batch")
    c = lax.axis_index("corpus")
    k = c % 2
    me = b * corpus + c
    to_sib = {"corpus": c + 1 - 2 * k}
    own_rows, full_half = resid_ref.shape
    w = HV.shape[1]
    docs = own_rows // DOC_LEN
    fetch = pltpu.make_async_copy(
        hash_ref.at[:, pl.ds(pl.multiple_of(k * w, w), w)], HV, h_sem
    )
    fetch.start()

    def swap(buf, sems):
        return pltpu.make_async_remote_copy(
            src_ref=buf.at[0], dst_ref=buf.at[1], send_sem=sems.at[0], recv_sem=sems.at[1],
            device_id=to_sib, device_id_type=pl.DeviceIdType.MESH,
        )

    square = jnp.sum(resid_ref[...] * resid_ref[...], axis=1, keepdims=True)
    SQ[0] = jnp.broadcast_to(square, SQ.shape[1:])
    swap(SQ, q_sem).start()
    swap(SQ, q_sem).wait()
    scale = lax.rsqrt((square + SQ[1][:, :1]) / float(2 * full_half) + 1e-06)
    final = resid_ref[...] * scale * gain_ref[...]
    pooled = [
        jnp.mean(final[d * DOC_LEN : (d + 1) * DOC_LEN], axis=0, keepdims=True)
        for d in range(docs)
    ]
    pooled.append(jnp.zeros((PB.shape[1] - docs, full_half), jnp.float32))
    PB[0] = jnp.concatenate(pooled, axis=0).astype(jnp.bfloat16)
    swap(PB, p_sem).start()
    fetch.wait()
    swap(PB, p_sem).wait()
    total = None
    parts = lax.axis_size("batch")
    span = full_half // parts
    for n in range(parts):
        for side in range(2):
            core = k if side == 0 else 1 - k
            term = jnp.dot(
                PB[side, :, n * span : (n + 1) * span],
                HV[pl.ds(pl.multiple_of(n * 2 * span + core * span, span), span), :],
                preferred_element_type=jnp.float32,
            )
            total = term if total is None else total + term
    codes = jnp.tanh(total)[:docs]
    lanes = CA.shape[2]
    CA[me] = jnp.concatenate(
        [codes[:, q * lanes : (q + 1) * lanes] for q in range(w // lanes)], axis=0
    ).astype(jnp.bfloat16)

    def tell(step):
        to = lax.rem(me + step, devices)
        return pltpu.make_async_remote_copy(
            src_ref=CA.at[me], dst_ref=CA.at[me],
            send_sem=a_send.at[step - 1], recv_sem=a_recv.at[step - 1],
            device_id={"batch": to // corpus, "corpus": to % corpus},
            device_id_type=pl.DeviceIdType.MESH,
        )

    def heard(step):
        src = lax.rem(me + devices - step, devices)
        return pltpu.make_async_remote_copy(
            src_ref=CA.at[src], dst_ref=CA.at[src],
            send_sem=a_send.at[step - 1], recv_sem=a_recv.at[step - 1],
            device_id={"batch": src // corpus, "corpus": src % corpus},
            device_id_type=pl.DeviceIdType.MESH,
        )

    @pl.loop(1, devices)
    def _(step):
        tell(step).start()

    @pl.loop(1, devices)
    def _(step):
        heard(step).wait_recv()

    @pl.loop(1, devices)
    def _(step):
        tell(step).wait_send()

    out_ref[...] = CA[...]


def all_codes(resid, final_gain, hash_weight):
    parts = lax.axis_size("batch")
    corpus = lax.axis_size("corpus")
    devices = parts * corpus
    own_rows, full_half = resid.shape
    docs = own_rows // DOC_LEN
    bits = hash_weight.shape[1]
    w = bits // 2
    gain = lax.dynamic_index_in_dim(
        final_gain.reshape(parts, 2, full_half // parts), lax.axis_index("corpus") % 2, 1, False
    ).reshape(1, full_half)
    vmem = pl.BlockSpec(memory_space=pltpu.VMEM)
    dma = pltpu.SemaphoreType.DMA
    groups = w // 128
    got = pl.pallas_call(
        code_kernel,
        out_shape=jax.ShapeDtypeStruct((devices, groups * docs, 128), jnp.bfloat16),
        in_specs=[vmem, vmem, pl.BlockSpec(memory_space=pl.ANY)],
        out_specs=vmem,
        scratch_shapes=[
            pltpu.VMEM((2 * full_half, w), jnp.bfloat16),
            pltpu.VMEM((2, own_rows, 128), jnp.float32),
            pltpu.VMEM((2, 16, full_half), jnp.bfloat16),
            pltpu.VMEM((devices, groups * docs, 128), jnp.bfloat16),
            dma, dma((2,)), dma((2,)), dma((devices - 1,)), dma((devices - 1,)),
        ],
        compiler_params=pltpu.CompilerParams(
            has_side_effects=True, vmem_limit_bytes=40 * 1024 * 1024
        ),
    )(resid, gain, hash_weight)
    got = got.reshape(parts, corpus // 2, 2, groups, docs, 128)
    return got.transpose(0, 1, 4, 2, 3, 5).reshape(devices // 2 * docs, bits)


def plain_codes(
    states, norm_gain, gate_weight, up_weight, down_weight, final_gain, hash_weight
):
    whole = lax.all_gather(states, "corpus", axis=1, tiled=True)
    normed = rms(whole.astype(jnp.float32), norm_gain).astype(jnp.bfloat16)

    def add_one(piece):
        return add_rows(normed, piece)

    gate = add_one(lax.all_gather(gate_weight, "batch", axis=0, tiled=True))
    up = add_one(lax.all_gather(up_weight, "batch", axis=0, tiled=True))
    hidden = (jax.nn.silu(gate) * up).astype(jnp.bfloat16)
    terms = jnp.dot(
        hidden,
        lax.all_gather(down_weight, "batch", axis=1, tiled=True),
        preferred_element_type=jnp.float32,
    )
    ffn = lax.psum_scatter(
        terms.astype(jnp.bfloat16), "corpus", scatter_dimension=0, tiled=True
    ).astype(jnp.float32)
    own_rows = ffn.shape[0]
    mine = lax.dynamic_slice_in_dim(whole, lax.axis_index("corpus") * own_rows, own_rows, 0)
    resid = mine.astype(jnp.float32) + ffn
    finals = rms(resid, final_gain)
    owned_docs = own_rows // DOC_LEN
    pooled = jnp.mean(finals.reshape(owned_docs, DOC_LEN, finals.shape[1]), axis=1).astype(
        jnp.bfloat16
    )
    codes = jnp.tanh(jnp.dot(pooled, hash_weight, preferred_element_type=jnp.float32)).astype(
        jnp.bfloat16
    )
    return lax.all_gather(codes, ("batch", "corpus"), axis=0, tiled=True)


def local(
    states,
    norm_gain,
    gate_weight,
    up_weight,
    down_weight,
    final_gain,
    hash_weight,
    query_bits,
    slot_map,
    query_index,
):
    corpus_count = lax.axis_size("corpus")
    devices = lax.axis_size("batch") * corpus_count
    flat_index = lax.axis_index("batch") * corpus_count + lax.axis_index("corpus")
    layer = (states, norm_gain, gate_weight, up_weight, down_weight)
    if lax.axis_size("batch") == 4 and corpus_count == 8:
        gathered = all_codes(wide(*layer), final_gain, hash_weight)
    else:
        gathered = plain_codes(*layer, final_gain, hash_weight)
    doc_total = gathered.shape[0]
    placing = (slot_map[:, None] == jnp.arange(doc_total, dtype=jnp.int32)[None, :]).astype(
        jnp.bfloat16
    )
    corpus = jnp.einsum("ds,dc->sc", placing, gathered, preferred_element_type=jnp.float32).astype(
        jnp.bfloat16
    )
    query_rows = NQ // devices
    my_bits = lax.dynamic_slice_in_dim(query_bits, flat_index * query_rows, query_rows, 0)
    my_index = lax.dynamic_slice_in_dim(query_index, flat_index * query_rows, query_rows, 0)
    return score(my_bits, corpus, my_index)


def solution(mesh):
    placed = (
        P("batch", "corpus"),
        P(),
        P("batch", "corpus"),
        P("batch", "corpus"),
        P("corpus", "batch"),
        P(),
        P(),
        P(),
        P(),
        P(),
    )
    return jax.shard_map(
        local, mesh=mesh, in_specs=placed, out_specs=P(("batch", "corpus"), None), check_vma=False
    )
```

```python
import jax
import jax.numpy as jnp
from jax import lax
from jax.experimental import pallas as pl
from jax.experimental.pallas import tpu as pltpu
from jax.sharding import PartitionSpec as P

DOC_LEN = 64
CODE = 1024
NQ = 4096


def rms(values, gain):
    return values * lax.rsqrt(jnp.mean(values * values, axis=-1, keepdims=True) + 1e-06) * gain


def add_rows(left, piece):
    return jnp.dot(left, piece, preferred_element_type=jnp.float32)


def score_kernel(bits_ref, corpus_ref, index_ref, out_ref):
    table = lax.dot_general(
        bits_ref[...],
        corpus_ref[...],
        (((1,), (1,)), ((), ())),
        preferred_element_type=jnp.float32,
    ) * (1.0 / float(bits_ref.shape[1]) ** 0.5)
    out_ref[...] = jnp.take_along_axis(table, index_ref[...], axis=1)


def score(bits, corpus, index):
    rows, top = index.shape
    lanes = 128 * max(pl.cdiv(corpus.shape[0], 128), pl.cdiv(top, 128))
    corpus = jnp.pad(corpus, ((0, lanes - corpus.shape[0]), (0, 0)))
    index = jnp.pad(index, ((0, 0), (0, lanes - top)))
    wide = pl.pallas_call(
        score_kernel, out_shape=jax.ShapeDtypeStruct((rows, lanes), jnp.float32)
    )(bits, corpus, index)
    return wide[:, :top]


def wide_kernel(
    states_ref, gain_ref, gate_ref, up_ref, down_ref, out_ref,
    X, G, U, W, AG, AU, H, SR, YR, ZR,
    s_loc, s_y, s_zr, s_zl, s_sib, w_loc, w_x, w_y, w_r, c_sib, c_y, c_z,
):
    nz = lax.axis_size("corpus") // 2
    b = lax.axis_index("batch")
    c = lax.axis_index("corpus")
    y, x = b // 2, b % 2
    z, k = c // 2, c % 2
    rows, feat = states_ref.shape
    half = W.shape[0]
    full = X.shape[1]
    cols = down_ref.shape[1]
    w = cols // 2
    by, bx, bd = (1 - y) * 2 + x, y * 2 + (1 - x), (1 - y) * 2 + (1 - x)
    to_y = {"batch": by}
    to_x = {"batch": bx}
    to_sib = {"corpus": z * 2 + (1 - k)}

    def at_z(other):
        return {"corpus": other * 2 + k}

    def remote(src, dst, sems, place):
        return pltpu.make_async_remote_copy(
            src_ref=src, dst_ref=dst, send_sem=sems.at[0], recv_sem=sems.at[1],
            device_id=place, device_id_type=pl.DeviceIdType.MESH,
        )

    def spot(t, zs, ks):
        block = y if t == 0 else 1 - y
        return X.at[
            pl.ds(pl.multiple_of(block * rows, rows), rows),
            pl.ds(pl.multiple_of((zs * 2 + ks) * feat, feat), feat),
        ]

    own_states = pltpu.make_async_copy(states_ref, spot(0, z, k), s_loc)
    y_states = remote(states_ref, X.at[
        pl.ds(pl.multiple_of(y * rows, rows), rows),
        pl.ds(pl.multiple_of(c * feat, feat), feat),
    ], s_y, to_y)

    def right(t, s):
        src = states_ref if t == 0 and s == 0 else spot(t, z - s, k)
        return remote(src, spot(t, z - s, k), s_zr.at[t, s], at_z(z + 1))

    def left(t, s):
        src = states_ref if t == 0 and s == 0 else spot(t, z + s, k)
        return remote(src, spot(t, z + s, k), s_zl.at[t, s], at_z(z - 1))

    def sib(t, zs):
        return remote(spot(t, zs, k), spot(t, zs, k), s_sib.at[t, zs], to_sib)

    def sib_in(t, zs):
        return remote(spot(t, zs, 1 - k), spot(t, zs, 1 - k), s_sib.at[t, zs], to_sib)

    def first(t):
        @pl.when(z + 1 < nz)
        def _():
            right(t, 0).start()

        @pl.when(z >= 1)
        def _():
            left(t, 0).start()

        sib(t, z).start()

    def relay(t, s):
        @pl.when(z - 1 - s >= 0)
        def _():
            right(t, s).wait_recv()
            if s + 1 < nz - 1:
                @pl.when(z + 1 < nz)
                def _():
                    right(t, s + 1).start()
            sib(t, z - 1 - s).start()

        @pl.when(z + 1 + s < nz)
        def _():
            left(t, s).wait_recv()
            if s + 1 < nz - 1:
                @pl.when(z >= 1)
                def _():
                    left(t, s + 1).start()
            sib(t, z + 1 + s).start()

    def part(m, mine):
        h = pl.ds(pl.multiple_of((y if mine else 1 - y) * half, half), half)
        if m == 2:
            return down_ref.at[h, :]
        return (gate_ref, up_ref)[m].at[:, h]

    def place(m, block):
        if m == 2:
            return W.at[:, pl.ds(pl.multiple_of(block * cols, cols), cols)]
        return (G, U)[m].at[pl.ds(pl.multiple_of(block * rows_w, rows_w), rows_w), :]

    rows_w = gate_ref.shape[0]
    loc = [pltpu.make_async_copy(part(m, True), place(m, b), w_loc.at[m]) for m in range(3)]
    wx = [remote(part(m, True), place(m, b), w_x.at[m], to_x) for m in range(3)]
    wy = [remote(part(m, False), place(m, b), w_y.at[m], to_y) for m in range(3)]
    wr = [remote(place(m, by), place(m, by), w_r.at[m], to_x) for m in range(3)]

    def settle(t):
        for zs in range(nz):
            sib_in(t, zs).wait_recv()
            sib(t, zs).wait_send()
        for s in range(nz - 1):
            @pl.when((z - s >= 0) & (z + 1 < nz))
            def _():
                right(t, s).wait_send()

            @pl.when((z + s < nz) & (z >= 1))
            def _():
                left(t, s).wait_send()

    gain = gain_ref[...]
    strip = min(512, rows)
    tile = min(256, rows)
    step = half // 3 if half % 384 == 0 else 128
    blocks = [x, 2 + x, 1 - x, 2 + (1 - x)]
    own_rows = out_ref.shape[0]

    def norm(t):
        start = (y if t == 0 else 1 - y) * rows

        @pl.loop(0, rows // 32)
        def _(p):
            r = pl.ds(pl.multiple_of(start + p * 32, 32), 32)
            v = X[r, :].astype(jnp.float32)
            scale = lax.rsqrt(jnp.mean(v * v, axis=-1, keepdims=True) + 1e-06)
            X[r, :] = (v * scale * gain).astype(jnp.bfloat16)

    def block_product(block, order):
        depth = pl.ds(pl.multiple_of(block * rows_w, rows_w), rows_w)

        @pl.loop(0, rows // strip)
        def _(i):
            here = pl.ds(pl.multiple_of(i * strip, strip), strip)
            r = pl.ds(pl.multiple_of((1 - y) * rows + i * strip, strip), strip)

            @pl.loop(0, half // step)
            def _(j):
                h = pl.ds(pl.multiple_of(j * step, 128), step)
                g = jnp.dot(X[r, depth], G[depth, h], preferred_element_type=jnp.float32)
                u = jnp.dot(X[r, depth], U[depth, h], preferred_element_type=jnp.float32)
                if order > 0:
                    g = g + AG[here, h]
                    u = u + AU[here, h]
                if order < 3:
                    AG[here, h] = g
                    AU[here, h] = u
                else:
                    H[r, h] = (g * jax.nn.sigmoid(g) * u).astype(jnp.bfloat16)

    def own_product(low, high):
        @pl.loop(low, high)
        def _(i):
            r = pl.ds(pl.multiple_of(y * rows + i * tile, tile), tile)

            @pl.loop(0, half // step)
            def _(j):
                h = pl.ds(pl.multiple_of(j * step, 128), step)
                g = jnp.dot(X[r, :], G[:, h], preferred_element_type=jnp.float32)
                u = jnp.dot(X[r, :], U[:, h], preferred_element_type=jnp.float32)
                H[r, h] = (g * jax.nn.sigmoid(g) * u).astype(jnp.bfloat16)

    y_states.start()
    own_states.start()
    wx[0].start()
    for m in range(3):
        wy[m].start()
    wx[1].start()
    own_states.wait()
    first(0)
    for m in range(3):
        loc[m].start()
    y_states.wait_recv()
    first(1)
    for s in range(nz - 1):
        relay(1, s)
        if s == 0:
            wy[0].wait_recv()
            wr[0].start()
    wy[1].wait_recv()
    wr[1].start()
    relay(0, 0)
    settle(1)
    norm(1)
    for s in range(1, nz - 1):
        if s == nz - 2:
            for m in range(2):
                loc[m].wait()
            block_product(b, 0)
            block_product(by, 1)
            for m in range(2):
                wx[m].wait_recv()
            block_product(bx, 2)
            wy[2].wait_recv()

            @pl.when(y == 0)
            def _():
                wx[2].start()
                wr[2].start()

            @pl.when(y == 1)
            def _():
                wr[2].start()
                wx[2].start()

        relay(0, s)
    settle(0)
    for j in range(4):
        out_ref[:, pl.ds(pl.multiple_of(blocks[j] * w, w), w)] = X[
            pl.ds(pl.multiple_of(y * rows + z * own_rows, own_rows), own_rows),
            pl.ds(pl.multiple_of(blocks[j] * cols + k * w, w), w),
        ].astype(jnp.float32)
    norm(0)
    for m in range(2):
        wr[m].wait_recv()
    block_product(bd, 3)
    loc[2].wait()

    base = full // 2

    def down_cols(j, core):
        return pl.ds(pl.multiple_of(blocks[j] * cols + core * w, w), w)

    def block_rows(t):
        return pl.ds(pl.multiple_of((y if t == 0 else 1 - y) * rows, rows), rows)

    def sib_sum(t, j):
        return remote(
            X.at[block_rows(t), pl.ds(j * w, w)], SR.at[j, block_rows(t), :],
            c_sib.at[t, j], to_sib,
        )

    def y_sum(j):
        return remote(X.at[block_rows(1), pl.ds(base + j * w, w)], YR.at[j], c_y.at[j], to_y)

    def z_sum(j, dz):
        to = lax.rem(z + dz, nz)
        return remote(
            X.at[
                pl.ds(pl.multiple_of(y * rows + to * own_rows, own_rows), own_rows),
                pl.ds(base + j * w, w),
            ],
            ZR.at[j, dz - 1], c_z.at[j, dz - 1], at_z(to),
        )

    def strips(t):
        start = (y if t == 0 else 1 - y) * rows
        return lambda i: pl.ds(pl.multiple_of(start + i * strip, strip), strip)

    def step_a(t, j):
        @pl.loop(0, rows // strip)
        def _(i):
            r = strips(t)(i)
            X[r, pl.ds(j * w, w)] = jnp.dot(
                H[r, :], W[:, down_cols(j, 1 - k)], preferred_element_type=jnp.float32
            ).astype(jnp.bfloat16)

        sib_sum(t, j).start()

    def step_b(t, j):
        sib_sum(t, j).wait_recv()

        @pl.loop(0, rows // strip)
        def _(i):
            r = strips(t)(i)
            X[r, pl.ds(base + j * w, w)] = (
                jnp.dot(H[r, :], W[:, down_cols(j, k)], preferred_element_type=jnp.float32)
                + SR[j, r, :].astype(jnp.float32)
            ).astype(jnp.bfloat16)

        if t == 1:
            y_sum(j).start()

    def step_c(j):
        y_sum(j).wait_recv()

        @pl.loop(0, rows // own_rows)
        def _(i):
            r = pl.ds(pl.multiple_of(y * rows + i * own_rows, own_rows), own_rows)
            here = pl.ds(base + j * w, w)
            X[r, here] = (
                X[r, here].astype(jnp.float32)
                + YR[j, pl.ds(pl.multiple_of(i * own_rows, own_rows), own_rows), :].astype(jnp.float32)
            ).astype(jnp.bfloat16)

        for dz in range(1, nz):
            z_sum(j, dz).start()

    def step_e(j):
        here = pl.ds(pl.multiple_of(blocks[j] * w, w), w)
        total = out_ref[:, here] + X[
            pl.ds(pl.multiple_of(y * rows + z * own_rows, own_rows), own_rows), pl.ds(base + j * w, w)
        ].astype(jnp.float32)
        for dz in range(1, nz):
            z_sum(j, dz).wait_recv()
            total = total + ZR[j, dz - 1].astype(jnp.float32)
        out_ref[:, here] = total

    def down_from_x(low):
        @pl.when(y == (0 if low else 1))
        def _():
            wx[2].wait_recv()

        @pl.when(y == (1 if low else 0))
        def _():
            wr[2].wait_recv()

    tiles = rows // tile
    step_a(1, 0)
    step_a(1, 1)
    own_product(0, 1)
    step_b(1, 0)
    step_b(1, 1)
    own_product(1, tiles)
    step_a(0, 0)
    step_a(0, 1)
    down_from_x(True)
    step_a(1, 2)
    step_a(0, 2)
    step_b(0, 0)
    step_b(1, 2)
    step_c(0)
    step_b(0, 1)
    step_b(0, 2)
    step_c(1)
    down_from_x(False)
    step_a(1, 3)
    step_a(0, 3)
    step_b(1, 3)
    step_b(0, 3)
    step_e(0)
    step_c(2)
    step_e(1)
    step_c(3)
    step_e(2)
    step_e(3)
    for j in range(4):
        sib_sum(0, j).wait_send()
        sib_sum(1, j).wait_send()
        y_sum(j).wait_send()
        for dz in range(1, nz):
            z_sum(j, dz).wait_send()
    y_states.wait_send()
    for m in range(3):
        wx[m].wait_send()
        wy[m].wait_send()
        wr[m].wait_send()


def wide(states, norm_gain, gate_weight, up_weight, down_weight):
    nz = lax.axis_size("corpus") // 2
    rows, feat = states.shape
    full = norm_gain.shape[0]
    half = gate_weight.shape[1] // 2
    cols = down_weight.shape[1]
    w = cols // 2
    own_rows = rows // nz
    dma = pltpu.SemaphoreType.DMA
    any_spec = pl.BlockSpec(memory_space=pl.ANY)
    vmem = pl.BlockSpec(memory_space=pltpu.VMEM)
    return pl.pallas_call(
        wide_kernel,
        out_shape=jax.ShapeDtypeStruct((own_rows, full // 2), jnp.float32),
        in_specs=[any_spec, vmem, any_spec, any_spec, any_spec],
        out_specs=vmem,
        scratch_shapes=[
            pltpu.VMEM((2 * rows, full), jnp.bfloat16),
            pltpu.VMEM((full, half), jnp.bfloat16),
            pltpu.VMEM((full, half), jnp.bfloat16),
            pltpu.VMEM((half, full), jnp.bfloat16),
            pltpu.VMEM((rows, half), jnp.float32),
            pltpu.VMEM((rows, half), jnp.float32),
            pltpu.VMEM((2 * rows, half), jnp.bfloat16),
            pltpu.VMEM((4, 2 * rows, w), jnp.bfloat16),
            pltpu.VMEM((4, rows, w), jnp.bfloat16),
            pltpu.VMEM((4, nz - 1, own_rows, w), jnp.bfloat16),
            dma, dma((2,)), dma((2, nz - 1, 2)), dma((2, nz - 1, 2)), dma((2, nz, 2)),
            dma((3,)), dma((3, 2)), dma((3, 2)), dma((3, 2)),
            dma((2, 4, 2)), dma((4, 2)), dma((4, nz - 1, 2)),
        ],
        compiler_params=pltpu.CompilerParams(
            has_side_effects=True, vmem_limit_bytes=67043328
        ),
    )(states, norm_gain[None], gate_weight, up_weight, down_weight)


def code_kernel(resid_ref, gain_ref, hash_ref, out_ref, HV, SQ, PB, CA, h_sem, q_sem, p_sem, a_send, a_recv):
    corpus = lax.axis_size("corpus")
    devices = lax.axis_size("batch") * corpus
    b = lax.axis_index("batch")
    c = lax.axis_index("corpus")
    k = c % 2
    me = b * corpus + c
    to_sib = {"corpus": c + 1 - 2 * k}
    own_rows, full_half = resid_ref.shape
    w = HV.shape[1]
    docs = own_rows // DOC_LEN
    fetch = pltpu.make_async_copy(
        hash_ref.at[:, pl.ds(pl.multiple_of(k * w, w), w)], HV, h_sem
    )
    fetch.start()

    def swap(buf, sems):
        return pltpu.make_async_remote_copy(
            src_ref=buf.at[0], dst_ref=buf.at[1], send_sem=sems.at[0], recv_sem=sems.at[1],
            device_id=to_sib, device_id_type=pl.DeviceIdType.MESH,
        )

    square = jnp.sum(resid_ref[...] * resid_ref[...], axis=1, keepdims=True)
    SQ[0] = jnp.broadcast_to(square, SQ.shape[1:])
    swap(SQ, q_sem).start()
    swap(SQ, q_sem).wait()
    scale = lax.rsqrt((square + SQ[1][:, :1]) / float(2 * full_half) + 1e-06)
    final = resid_ref[...] * scale * gain_ref[...]
    pooled = [
        jnp.mean(final[d * DOC_LEN : (d + 1) * DOC_LEN], axis=0, keepdims=True)
        for d in range(docs)
    ]
    pooled.append(jnp.zeros((PB.shape[1] - docs, full_half), jnp.float32))
    PB[0] = jnp.concatenate(pooled, axis=0).astype(jnp.bfloat16)
    swap(PB, p_sem).start()
    fetch.wait()
    swap(PB, p_sem).wait()
    total = None
    parts = lax.axis_size("batch")
    span = full_half // parts
    for n in range(parts):
        for side in range(2):
            core = k if side == 0 else 1 - k
            term = jnp.dot(
                PB[side, :, n * span : (n + 1) * span],
                HV[pl.ds(pl.multiple_of(n * 2 * span + core * span, span), span), :],
                preferred_element_type=jnp.float32,
            )
            total = term if total is None else total + term
    codes = jnp.tanh(total)[:docs]
    lanes = CA.shape[2]
    CA[me] = jnp.concatenate(
        [codes[:, q * lanes : (q + 1) * lanes] for q in range(w // lanes)], axis=0
    ).astype(jnp.bfloat16)

    def tell(step):
        to = lax.rem(me + step, devices)
        return pltpu.make_async_remote_copy(
            src_ref=CA.at[me], dst_ref=CA.at[me],
            send_sem=a_send.at[step - 1], recv_sem=a_recv.at[step - 1],
            device_id={"batch": to // corpus, "corpus": to % corpus},
            device_id_type=pl.DeviceIdType.MESH,
        )

    def heard(step):
        src = lax.rem(me + devices - step, devices)
        return pltpu.make_async_remote_copy(
            src_ref=CA.at[src], dst_ref=CA.at[src],
            send_sem=a_send.at[step - 1], recv_sem=a_recv.at[step - 1],
            device_id={"batch": src // corpus, "corpus": src % corpus},
            device_id_type=pl.DeviceIdType.MESH,
        )

    @pl.loop(1, devices)
    def _(step):
        tell(step).start()

    @pl.loop(1, devices)
    def _(step):
        heard(step).wait_recv()

    @pl.loop(1, devices)
    def _(step):
        tell(step).wait_send()

    out_ref[...] = CA[...]


def all_codes(resid, final_gain, hash_weight):
    parts = lax.axis_size("batch")
    corpus = lax.axis_size("corpus")
    devices = parts * corpus
    own_rows, full_half = resid.shape
    docs = own_rows // DOC_LEN
    bits = hash_weight.shape[1]
    w = bits // 2
    gain = lax.dynamic_index_in_dim(
        final_gain.reshape(parts, 2, full_half // parts), lax.axis_index("corpus") % 2, 1, False
    ).reshape(1, full_half)
    vmem = pl.BlockSpec(memory_space=pltpu.VMEM)
    dma = pltpu.SemaphoreType.DMA
    groups = w // 128
    got = pl.pallas_call(
        code_kernel,
        out_shape=jax.ShapeDtypeStruct((devices, groups * docs, 128), jnp.bfloat16),
        in_specs=[vmem, vmem, pl.BlockSpec(memory_space=pl.ANY)],
        out_specs=vmem,
        scratch_shapes=[
            pltpu.VMEM((2 * full_half, w), jnp.bfloat16),
            pltpu.VMEM((2, own_rows, 128), jnp.float32),
            pltpu.VMEM((2, 16, full_half), jnp.bfloat16),
            pltpu.VMEM((devices, groups * docs, 128), jnp.bfloat16),
            dma, dma((2,)), dma((2,)), dma((devices - 1,)), dma((devices - 1,)),
        ],
        compiler_params=pltpu.CompilerParams(
            has_side_effects=True, vmem_limit_bytes=67043328
        ),
    )(resid, gain, hash_weight)
    got = got.reshape(parts, corpus // 2, 2, groups, docs, 128)
    return got.transpose(0, 1, 4, 2, 3, 5).reshape(devices // 2 * docs, bits)


def plain_codes(
    states, norm_gain, gate_weight, up_weight, down_weight, final_gain, hash_weight
):
    whole = lax.all_gather(states, "corpus", axis=1, tiled=True)
    normed = rms(whole.astype(jnp.float32), norm_gain).astype(jnp.bfloat16)

    def add_one(piece):
        return add_rows(normed, piece)

    gate = add_one(lax.all_gather(gate_weight, "batch", axis=0, tiled=True))
    up = add_one(lax.all_gather(up_weight, "batch", axis=0, tiled=True))
    hidden = (jax.nn.silu(gate) * up).astype(jnp.bfloat16)
    terms = jnp.dot(
        hidden,
        lax.all_gather(down_weight, "batch", axis=1, tiled=True),
        preferred_element_type=jnp.float32,
    )
    ffn = lax.psum_scatter(
        terms.astype(jnp.bfloat16), "corpus", scatter_dimension=0, tiled=True
    ).astype(jnp.float32)
    own_rows = ffn.shape[0]
    mine = lax.dynamic_slice_in_dim(whole, lax.axis_index("corpus") * own_rows, own_rows, 0)
    resid = mine.astype(jnp.float32) + ffn
    finals = rms(resid, final_gain)
    owned_docs = own_rows // DOC_LEN
    pooled = jnp.mean(finals.reshape(owned_docs, DOC_LEN, finals.shape[1]), axis=1).astype(
        jnp.bfloat16
    )
    codes = jnp.tanh(jnp.dot(pooled, hash_weight, preferred_element_type=jnp.float32)).astype(
        jnp.bfloat16
    )
    return lax.all_gather(codes, ("batch", "corpus"), axis=0, tiled=True)


def local(
    states,
    norm_gain,
    gate_weight,
    up_weight,
    down_weight,
    final_gain,
    hash_weight,
    query_bits,
    slot_map,
    query_index,
):
    corpus_count = lax.axis_size("corpus")
    devices = lax.axis_size("batch") * corpus_count
    flat_index = lax.axis_index("batch") * corpus_count + lax.axis_index("corpus")
    layer = (states, norm_gain, gate_weight, up_weight, down_weight)
    if lax.axis_size("batch") == 4 and corpus_count == 8:
        gathered = all_codes(wide(*layer), final_gain, hash_weight)
    else:
        gathered = plain_codes(*layer, final_gain, hash_weight)
    doc_total = gathered.shape[0]
    placing = (slot_map[:, None] == jnp.arange(doc_total, dtype=jnp.int32)[None, :]).astype(
        jnp.bfloat16
    )
    corpus = jnp.einsum("ds,dc->sc", placing, gathered, preferred_element_type=jnp.float32).astype(
        jnp.bfloat16
    )
    query_rows = NQ // devices
    my_bits = lax.dynamic_slice_in_dim(query_bits, flat_index * query_rows, query_rows, 0)
    my_index = lax.dynamic_slice_in_dim(query_index, flat_index * query_rows, query_rows, 0)
    return score(my_bits, corpus, my_index)


def solution(mesh):
    placed = (
        P("batch", "corpus"),
        P(),
        P("batch", "corpus"),
        P("batch", "corpus"),
        P("corpus", "batch"),
        P(),
        P(),
        P(),
        P(),
        P(),
    )
    return jax.shard_map(
        local, mesh=mesh, in_specs=placed, out_specs=P(("batch", "corpus"), None), check_vma=False
    )
```

```python
import jax
import jax.numpy as jnp
from jax import lax
from jax.experimental import pallas as pl
from jax.experimental.pallas import tpu as pltpu
from jax.sharding import PartitionSpec as P

DOC_LEN = 64


def rms(values, gain):
    return values * lax.rsqrt(jnp.mean(values * values, axis=-1, keepdims=True) + 1e-06) * gain


def add_rows(left, piece):
    return jnp.dot(left, piece, preferred_element_type=jnp.float32)


def score_kernel(place_ref, bits_ref, codes_ref, slot_ref, index_ref, out_ref, picks):
    docs = codes_ref.shape[0]
    lanes = picks.shape[1]
    top = index_ref.shape[1]
    entry = lax.broadcasted_iota(jnp.int32, (lanes, docs), 0)
    placing = jnp.where(entry == slot_ref[...], 1.0, 0.0).astype(jnp.bfloat16)
    corpus = jnp.dot(placing, codes_ref[...], preferred_element_type=jnp.float32).astype(
        jnp.bfloat16
    )
    table = lax.dot_general(
        bits_ref[...],
        corpus,
        (((1,), (1,)), ((), ())),
        preferred_element_type=jnp.float32,
    ) * (1.0 / float(bits_ref.shape[1]) ** 0.5)
    picks[...] = jnp.zeros_like(picks)
    picks[:, :top] = index_ref[...]
    out_ref[...] = jnp.take_along_axis(table, picks[...], axis=1)[:, :top]


def score(query_bits, codes, slot_map, query_index, flat_index, rows):
    docs, bits = codes.shape
    top = query_index.shape[1]
    lanes = 128 * max(pl.cdiv(docs, 128), pl.cdiv(top, 128))
    return pl.pallas_call(
        score_kernel,
        out_shape=jax.ShapeDtypeStruct((rows, top), jnp.float32),
        grid_spec=pltpu.PrefetchScalarGridSpec(
            num_scalar_prefetch=1,
            grid=(1,),
            in_specs=[
                pl.BlockSpec((rows, bits), lambda i, f: (f[0], 0)),
                pl.BlockSpec((docs, bits), lambda i, f: (0, 0)),
                pl.BlockSpec((1, docs), lambda i, f: (0, 0)),
                pl.BlockSpec((rows, top), lambda i, f: (f[0], 0)),
            ],
            out_specs=pl.BlockSpec((rows, top), lambda i, f: (0, 0)),
            scratch_shapes=[pltpu.VMEM((rows, lanes), jnp.int32)],
        ),
    )(flat_index.reshape(1), query_bits, codes, slot_map[None], query_index)


def wide_kernel(
    states_ref, gain_ref, gate_ref, up_ref, down_ref, out_ref,
    X, G, U, W, AG, AU, H, SR, YR, ZR,
    s_loc, s_y, s_zr, s_zl, s_sib, w_loc, w_x, w_y, w_r, c_sib, c_y, c_z,
):
    nz = lax.axis_size("corpus") // 2
    b = lax.axis_index("batch")
    c = lax.axis_index("corpus")
    y, x = b // 2, b % 2
    z, k = c // 2, c % 2
    rows, feat = states_ref.shape
    half = W.shape[0]
    full = X.shape[1]
    cols = down_ref.shape[1]
    w = cols // 2
    by, bx, bd = (1 - y) * 2 + x, y * 2 + (1 - x), (1 - y) * 2 + (1 - x)
    to_y = {"batch": by}
    to_x = {"batch": bx}
    to_sib = {"corpus": z * 2 + (1 - k)}

    def at_z(other):
        return {"corpus": other * 2 + k}

    def remote(src, dst, sems, place):
        return pltpu.make_async_remote_copy(
            src_ref=src, dst_ref=dst, send_sem=sems.at[0], recv_sem=sems.at[1],
            device_id=place, device_id_type=pl.DeviceIdType.MESH,
        )

    def spot(t, zs, ks):
        block = y if t == 0 else 1 - y
        return X.at[
            pl.ds(pl.multiple_of(block * rows, rows), rows),
            pl.ds(pl.multiple_of((zs * 2 + ks) * feat, feat), feat),
        ]

    own_states = pltpu.make_async_copy(states_ref, spot(0, z, k), s_loc)
    y_states = remote(states_ref, X.at[
        pl.ds(pl.multiple_of(y * rows, rows), rows),
        pl.ds(pl.multiple_of(c * feat, feat), feat),
    ], s_y, to_y)

    def right(t, s):
        src = states_ref if t == 0 and s == 0 else spot(t, z - s, k)
        return remote(src, spot(t, z - s, k), s_zr.at[t, s], at_z(z + 1))

    def left(t, s):
        src = states_ref if t == 0 and s == 0 else spot(t, z + s, k)
        return remote(src, spot(t, z + s, k), s_zl.at[t, s], at_z(z - 1))

    def sib(t, zs):
        return remote(spot(t, zs, k), spot(t, zs, k), s_sib.at[t, zs], to_sib)

    def sib_in(t, zs):
        return remote(spot(t, zs, 1 - k), spot(t, zs, 1 - k), s_sib.at[t, zs], to_sib)

    def first(t):
        @pl.when(z + 1 < nz)
        def _():
            right(t, 0).start()

        @pl.when(z >= 1)
        def _():
            left(t, 0).start()

        sib(t, z).start()

    def relay(t, s):
        @pl.when(z - 1 - s >= 0)
        def _():
            right(t, s).wait_recv()
            if s + 1 < nz - 1:
                @pl.when(z + 1 < nz)
                def _():
                    right(t, s + 1).start()
            sib(t, z - 1 - s).start()

        @pl.when(z + 1 + s < nz)
        def _():
            left(t, s).wait_recv()
            if s + 1 < nz - 1:
                @pl.when(z >= 1)
                def _():
                    left(t, s + 1).start()
            sib(t, z + 1 + s).start()

    def part(m, mine):
        h = pl.ds(pl.multiple_of((y if mine else 1 - y) * half, half), half)
        if m == 2:
            return down_ref.at[h, :]
        return (gate_ref, up_ref)[m].at[:, h]

    def place(m, block):
        if m == 2:
            return W.at[:, pl.ds(pl.multiple_of(block * cols, cols), cols)]
        return (G, U)[m].at[pl.ds(pl.multiple_of(block * rows_w, rows_w), rows_w), :]

    rows_w = gate_ref.shape[0]
    loc = [pltpu.make_async_copy(part(m, True), place(m, b), w_loc.at[m]) for m in range(3)]
    wx = [remote(part(m, True), place(m, b), w_x.at[m], to_x) for m in range(3)]
    wy = [remote(part(m, False), place(m, b), w_y.at[m], to_y) for m in range(3)]
    wr = [remote(place(m, by), place(m, by), w_r.at[m], to_x) for m in range(3)]

    def settle(t):
        for zs in range(nz):
            sib_in(t, zs).wait_recv()
            sib(t, zs).wait_send()
        for s in range(nz - 1):
            @pl.when((z - s >= 0) & (z + 1 < nz))
            def _():
                right(t, s).wait_send()

            @pl.when((z + s < nz) & (z >= 1))
            def _():
                left(t, s).wait_send()

    gain = gain_ref[...]
    strip = min(512, rows)
    tile = min(256, rows)
    step = half // 3 if half % 384 == 0 else 128
    blocks = [x, 2 + x, 1 - x, 2 + (1 - x)]
    own_rows = out_ref.shape[0]

    def norm(t):
        start = (y if t == 0 else 1 - y) * rows

        @pl.loop(0, rows // 32)
        def _(p):
            r = pl.ds(pl.multiple_of(start + p * 32, 32), 32)
            v = X[r, :].astype(jnp.float32)
            scale = lax.rsqrt(jnp.mean(v * v, axis=-1, keepdims=True) + 1e-06)
            X[r, :] = (v * scale * gain).astype(jnp.bfloat16)

    def block_product(block, order):
        depth = pl.ds(pl.multiple_of(block * rows_w, rows_w), rows_w)

        @pl.loop(0, rows // strip)
        def _(i):
            here = pl.ds(pl.multiple_of(i * strip, strip), strip)
            r = pl.ds(pl.multiple_of((1 - y) * rows + i * strip, strip), strip)

            @pl.loop(0, half // step)
            def _(j):
                h = pl.ds(pl.multiple_of(j * step, 128), step)
                g = jnp.dot(X[r, depth], G[depth, h], preferred_element_type=jnp.float32)
                u = jnp.dot(X[r, depth], U[depth, h], preferred_element_type=jnp.float32)
                if order > 0:
                    g = g + AG[here, h]
                    u = u + AU[here, h]
                if order < 3:
                    AG[here, h] = g
                    AU[here, h] = u
                else:
                    H[r, h] = (g * jax.nn.sigmoid(g) * u).astype(jnp.bfloat16)

    def own_product(low, high):
        @pl.loop(low, high)
        def _(i):
            r = pl.ds(pl.multiple_of(y * rows + i * tile, tile), tile)

            @pl.loop(0, half // step)
            def _(j):
                h = pl.ds(pl.multiple_of(j * step, 128), step)
                g = jnp.dot(X[r, :], G[:, h], preferred_element_type=jnp.float32)
                u = jnp.dot(X[r, :], U[:, h], preferred_element_type=jnp.float32)
                H[r, h] = (g * jax.nn.sigmoid(g) * u).astype(jnp.bfloat16)

    y_states.start()
    own_states.start()
    wx[0].start()
    for m in range(3):
        wy[m].start()
    wx[1].start()
    own_states.wait()
    first(0)
    for m in range(3):
        loc[m].start()
    y_states.wait_recv()
    first(1)
    for s in range(nz - 1):
        relay(1, s)
        if s == 0:
            wy[0].wait_recv()
            wr[0].start()
    wy[1].wait_recv()
    wr[1].start()
    relay(0, 0)
    settle(1)
    norm(1)
    for s in range(1, nz - 1):
        if s == nz - 2:
            for m in range(2):
                loc[m].wait()
            block_product(b, 0)
            block_product(by, 1)
            for m in range(2):
                wx[m].wait_recv()
            block_product(bx, 2)
            wy[2].wait_recv()

            @pl.when(y == 0)
            def _():
                wx[2].start()
                wr[2].start()

            @pl.when(y == 1)
            def _():
                wr[2].start()
                wx[2].start()

        relay(0, s)
    settle(0)
    for j in range(4):
        out_ref[:, pl.ds(pl.multiple_of(blocks[j] * w, w), w)] = X[
            pl.ds(pl.multiple_of(y * rows + z * own_rows, own_rows), own_rows),
            pl.ds(pl.multiple_of(blocks[j] * cols + k * w, w), w),
        ].astype(jnp.float32)
    norm(0)
    for m in range(2):
        wr[m].wait_recv()
    block_product(bd, 3)
    loc[2].wait()

    base = full // 2

    def down_cols(j, core):
        return pl.ds(pl.multiple_of(blocks[j] * cols + core * w, w), w)

    def block_rows(t):
        return pl.ds(pl.multiple_of((y if t == 0 else 1 - y) * rows, rows), rows)

    def sib_sum(t, j):
        return remote(
            X.at[block_rows(t), pl.ds(j * w, w)], SR.at[j, block_rows(t), :],
            c_sib.at[t, j], to_sib,
        )

    hw = w // 2

    def y_sum(j, h):
        return remote(
            X.at[block_rows(1), pl.ds(base + j * w + h * hw, hw)],
            YR.at[j, :, pl.ds(h * hw, hw)], c_y.at[j, h], to_y,
        )

    def z_sum(j, h, dz):
        to = lax.rem(z + dz, nz)
        return remote(
            X.at[
                pl.ds(pl.multiple_of(y * rows + to * own_rows, own_rows), own_rows),
                pl.ds(base + j * w + h * hw, hw),
            ],
            ZR.at[j, dz - 1, :, pl.ds(h * hw, hw)], c_z.at[j, h, dz - 1], at_z(to),
        )

    def strips(t):
        start = (y if t == 0 else 1 - y) * rows
        return lambda i: pl.ds(pl.multiple_of(start + i * strip, strip), strip)

    def step_a(t, j):
        @pl.loop(0, rows // strip)
        def _(i):
            r = strips(t)(i)
            X[r, pl.ds(j * w, w)] = jnp.dot(
                H[r, :], W[:, down_cols(j, 1 - k)], preferred_element_type=jnp.float32
            ).astype(jnp.bfloat16)

        sib_sum(t, j).start()

    def step_b(t, j):
        sib_sum(t, j).wait_recv()
        for h in range(2):
            down = pl.ds(pl.multiple_of(blocks[j] * cols + k * w + h * hw, hw), hw)

            @pl.loop(0, rows // strip)
            def _(i):
                r = strips(t)(i)
                X[r, pl.ds(base + j * w + h * hw, hw)] = (
                    jnp.dot(H[r, :], W[:, down], preferred_element_type=jnp.float32)
                    + SR[j, r, pl.ds(h * hw, hw)].astype(jnp.float32)
                ).astype(jnp.bfloat16)

            if t == 1:
                y_sum(j, h).start()

    def half_c(j, h):
        y_sum(j, h).wait_recv()

        @pl.loop(0, rows // own_rows)
        def _(i):
            r = pl.ds(pl.multiple_of(y * rows + i * own_rows, own_rows), own_rows)
            here = pl.ds(base + j * w + h * hw, hw)
            q = pl.ds(pl.multiple_of(i * own_rows, own_rows), own_rows)
            X[r, here] = (
                X[r, here].astype(jnp.float32)
                + YR[j, q, pl.ds(h * hw, hw)].astype(jnp.float32)
            ).astype(jnp.bfloat16)

        for dz in range(1, nz):
            z_sum(j, h, dz).start()

    def step_c(j):
        half_c(j, 0)
        half_c(j, 1)

    def half_e(j, h):
        here = pl.ds(pl.multiple_of(blocks[j] * w + h * hw, hw), hw)
        total = out_ref[:, here] + X[
            pl.ds(pl.multiple_of(y * rows + z * own_rows, own_rows), own_rows),
            pl.ds(base + j * w + h * hw, hw),
        ].astype(jnp.float32)
        for dz in range(1, nz):
            z_sum(j, h, dz).wait_recv()
            total = total + ZR[j, dz - 1, :, pl.ds(h * hw, hw)].astype(jnp.float32)
        out_ref[:, here] = total

    def step_e(j):
        half_e(j, 0)
        half_e(j, 1)

    def down_from_x(low):
        @pl.when(y == (0 if low else 1))
        def _():
            wx[2].wait_recv()

        @pl.when(y == (1 if low else 0))
        def _():
            wr[2].wait_recv()

    tiles = rows // tile
    step_a(1, 0)
    step_a(1, 1)
    own_product(0, 1)
    step_b(1, 0)
    step_b(1, 1)
    own_product(1, tiles)
    step_a(0, 0)
    step_a(0, 1)
    down_from_x(True)
    step_a(1, 2)
    step_a(0, 2)
    step_b(0, 0)
    step_b(1, 2)
    step_c(0)
    step_b(0, 1)
    step_b(0, 2)
    step_c(1)
    down_from_x(False)
    step_a(1, 3)
    step_a(0, 3)
    step_b(1, 3)
    step_b(0, 3)
    step_e(0)
    step_c(2)
    half_c(3, 0)
    step_e(1)
    half_c(3, 1)
    step_e(2)
    step_e(3)
    for j in range(4):
        sib_sum(0, j).wait_send()
        sib_sum(1, j).wait_send()
        for h in range(2):
            y_sum(j, h).wait_send()
            for dz in range(1, nz):
                z_sum(j, h, dz).wait_send()
    y_states.wait_send()
    for m in range(3):
        wx[m].wait_send()
        wy[m].wait_send()
        wr[m].wait_send()


def wide(states, norm_gain, gate_weight, up_weight, down_weight):
    nz = lax.axis_size("corpus") // 2
    rows, feat = states.shape
    full = norm_gain.shape[0]
    half = gate_weight.shape[1] // 2
    cols = down_weight.shape[1]
    w = cols // 2
    own_rows = rows // nz
    dma = pltpu.SemaphoreType.DMA
    any_spec = pl.BlockSpec(memory_space=pl.ANY)
    vmem = pl.BlockSpec(memory_space=pltpu.VMEM)
    return pl.pallas_call(
        wide_kernel,
        out_shape=jax.ShapeDtypeStruct((own_rows, full // 2), jnp.float32),
        in_specs=[any_spec, vmem, any_spec, any_spec, any_spec],
        out_specs=vmem,
        scratch_shapes=[
            pltpu.VMEM((2 * rows, full), jnp.bfloat16),
            pltpu.VMEM((full, half), jnp.bfloat16),
            pltpu.VMEM((full, half), jnp.bfloat16),
            pltpu.VMEM((half, full), jnp.bfloat16),
            pltpu.VMEM((rows, half), jnp.float32),
            pltpu.VMEM((rows, half), jnp.float32),
            pltpu.VMEM((2 * rows, half), jnp.bfloat16),
            pltpu.VMEM((4, 2 * rows, w), jnp.bfloat16),
            pltpu.VMEM((4, rows, w), jnp.bfloat16),
            pltpu.VMEM((4, nz - 1, own_rows, w), jnp.bfloat16),
            dma, dma((2,)), dma((2, nz - 1, 2)), dma((2, nz - 1, 2)), dma((2, nz, 2)),
            dma((3,)), dma((3, 2)), dma((3, 2)), dma((3, 2)),
            dma((2, 4, 2)), dma((4, 2, 2)), dma((4, 2, nz - 1, 2)),
        ],
        compiler_params=pltpu.CompilerParams(
            has_side_effects=True, vmem_limit_bytes=67043328
        ),
    )(states, norm_gain[None], gate_weight, up_weight, down_weight)


def code_kernel(resid_ref, gain_ref, hash_ref, out_ref, HV, SQ, PB, CA, h_sem, q_sem, p_sem, a_send, a_recv):
    corpus = lax.axis_size("corpus")
    devices = lax.axis_size("batch") * corpus
    b = lax.axis_index("batch")
    c = lax.axis_index("corpus")
    k = c % 2
    me = b * corpus + c
    to_sib = {"corpus": c + 1 - 2 * k}
    own_rows, full_half = resid_ref.shape
    w = HV.shape[1]
    docs = own_rows // DOC_LEN
    fetch = pltpu.make_async_copy(
        hash_ref.at[:, pl.ds(pl.multiple_of(k * w, w), w)], HV, h_sem
    )
    fetch.start()

    def swap(buf, sems):
        return pltpu.make_async_remote_copy(
            src_ref=buf.at[0], dst_ref=buf.at[1], send_sem=sems.at[0], recv_sem=sems.at[1],
            device_id=to_sib, device_id_type=pl.DeviceIdType.MESH,
        )

    square = jnp.sum(resid_ref[...] * resid_ref[...], axis=1, keepdims=True)
    SQ[0] = jnp.broadcast_to(square, SQ.shape[1:])
    swap(SQ, q_sem).start()
    swap(SQ, q_sem).wait()
    scale = lax.rsqrt((square + SQ[1][:, :1]) / float(2 * full_half) + 1e-06)
    final = resid_ref[...] * scale * gain_ref[...]
    pooled = [
        jnp.mean(final[d * DOC_LEN : (d + 1) * DOC_LEN], axis=0, keepdims=True)
        for d in range(docs)
    ]
    pooled.append(jnp.zeros((PB.shape[1] - docs, full_half), jnp.float32))
    PB[0] = jnp.concatenate(pooled, axis=0).astype(jnp.bfloat16)
    swap(PB, p_sem).start()
    fetch.wait()
    swap(PB, p_sem).wait()
    total = None
    parts = lax.axis_size("batch")
    span = full_half // parts
    for n in range(parts):
        for side in range(2):
            core = k if side == 0 else 1 - k
            term = jnp.dot(
                PB[side, :, n * span : (n + 1) * span],
                HV[pl.ds(pl.multiple_of(n * 2 * span + core * span, span), span), :],
                preferred_element_type=jnp.float32,
            )
            total = term if total is None else total + term
    codes = jnp.tanh(total)[:docs]
    lanes = CA.shape[2]
    CA[me] = jnp.concatenate(
        [codes[:, q * lanes : (q + 1) * lanes] for q in range(w // lanes)], axis=0
    ).astype(jnp.bfloat16)

    def tell(step):
        to = lax.rem(me + step, devices)
        return pltpu.make_async_remote_copy(
            src_ref=CA.at[me], dst_ref=CA.at[me],
            send_sem=a_send.at[step - 1], recv_sem=a_recv.at[step - 1],
            device_id={"batch": to // corpus, "corpus": to % corpus},
            device_id_type=pl.DeviceIdType.MESH,
        )

    def heard(step):
        src = lax.rem(me + devices - step, devices)
        return pltpu.make_async_remote_copy(
            src_ref=CA.at[src], dst_ref=CA.at[src],
            send_sem=a_send.at[step - 1], recv_sem=a_recv.at[step - 1],
            device_id={"batch": src // corpus, "corpus": src % corpus},
            device_id_type=pl.DeviceIdType.MESH,
        )

    @pl.loop(1, devices)
    def _(step):
        tell(step).start()

    @pl.loop(1, devices)
    def _(step):
        heard(step).wait_recv()

    @pl.loop(1, devices)
    def _(step):
        tell(step).wait_send()

    out_ref[...] = CA[...]


def all_codes(resid, final_gain, hash_weight):
    parts = lax.axis_size("batch")
    corpus = lax.axis_size("corpus")
    devices = parts * corpus
    own_rows, full_half = resid.shape
    docs = own_rows // DOC_LEN
    bits = hash_weight.shape[1]
    w = bits // 2
    gain = lax.dynamic_index_in_dim(
        final_gain.reshape(parts, 2, full_half // parts), lax.axis_index("corpus") % 2, 1, False
    ).reshape(1, full_half)
    vmem = pl.BlockSpec(memory_space=pltpu.VMEM)
    dma = pltpu.SemaphoreType.DMA
    groups = w // 128
    got = pl.pallas_call(
        code_kernel,
        out_shape=jax.ShapeDtypeStruct((devices, groups * docs, 128), jnp.bfloat16),
        in_specs=[vmem, vmem, pl.BlockSpec(memory_space=pl.ANY)],
        out_specs=vmem,
        scratch_shapes=[
            pltpu.VMEM((2 * full_half, w), jnp.bfloat16),
            pltpu.VMEM((2, own_rows, 128), jnp.float32),
            pltpu.VMEM((2, 16, full_half), jnp.bfloat16),
            pltpu.VMEM((devices, groups * docs, 128), jnp.bfloat16),
            dma, dma((2,)), dma((2,)), dma((devices - 1,)), dma((devices - 1,)),
        ],
        compiler_params=pltpu.CompilerParams(
            has_side_effects=True, vmem_limit_bytes=67043328
        ),
    )(resid, gain, hash_weight)
    got = got.reshape(parts, corpus // 2, 2, groups, docs, 128)
    return got.transpose(0, 1, 4, 2, 3, 5).reshape(devices // 2 * docs, bits)


def plain_codes(
    states, norm_gain, gate_weight, up_weight, down_weight, final_gain, hash_weight
):
    whole = lax.all_gather(states, "corpus", axis=1, tiled=True)
    normed = rms(whole.astype(jnp.float32), norm_gain).astype(jnp.bfloat16)

    def add_one(piece):
        return add_rows(normed, piece)

    gate = add_one(lax.all_gather(gate_weight, "batch", axis=0, tiled=True))
    up = add_one(lax.all_gather(up_weight, "batch", axis=0, tiled=True))
    hidden = (jax.nn.silu(gate) * up).astype(jnp.bfloat16)
    terms = jnp.dot(
        hidden,
        lax.all_gather(down_weight, "batch", axis=1, tiled=True),
        preferred_element_type=jnp.float32,
    )
    ffn = lax.psum_scatter(
        terms.astype(jnp.bfloat16), "corpus", scatter_dimension=0, tiled=True
    ).astype(jnp.float32)
    own_rows = ffn.shape[0]
    mine = lax.dynamic_slice_in_dim(whole, lax.axis_index("corpus") * own_rows, own_rows, 0)
    resid = mine.astype(jnp.float32) + ffn
    finals = rms(resid, final_gain)
    owned_docs = own_rows // DOC_LEN
    pooled = jnp.mean(finals.reshape(owned_docs, DOC_LEN, finals.shape[1]), axis=1).astype(
        jnp.bfloat16
    )
    codes = jnp.tanh(jnp.dot(pooled, hash_weight, preferred_element_type=jnp.float32)).astype(
        jnp.bfloat16
    )
    return lax.all_gather(codes, ("batch", "corpus"), axis=0, tiled=True)


def local(
    states,
    norm_gain,
    gate_weight,
    up_weight,
    down_weight,
    final_gain,
    hash_weight,
    query_bits,
    slot_map,
    query_index,
):
    corpus_count = lax.axis_size("corpus")
    devices = lax.axis_size("batch") * corpus_count
    flat_index = lax.axis_index("batch") * corpus_count + lax.axis_index("corpus")
    layer = (states, norm_gain, gate_weight, up_weight, down_weight)
    if lax.axis_size("batch") == 4 and corpus_count == 8:
        gathered = all_codes(wide(*layer), final_gain, hash_weight)
    else:
        gathered = plain_codes(*layer, final_gain, hash_weight)
    query_rows = query_bits.shape[0] // devices
    return score(query_bits, gathered, slot_map, query_index, flat_index, query_rows)


def solution(mesh):
    placed = (
        P("batch", "corpus"),
        P(),
        P("batch", "corpus"),
        P("batch", "corpus"),
        P("corpus", "batch"),
        P(),
        P(),
        P(),
        P(),
        P(),
    )
    return jax.shard_map(
        local, mesh=mesh, in_specs=placed, out_specs=P(("batch", "corpus"), None), check_vma=False
    )
```

```python
import jax
import jax.numpy as jnp
from jax import lax
from jax.experimental import pallas as pl
from jax.experimental.pallas import tpu as pltpu
from jax.sharding import PartitionSpec as P

DOC_LEN = 64


def rms(values, gain):
    return values * lax.rsqrt(jnp.mean(values * values, axis=-1, keepdims=True) + 1e-06) * gain


def add_rows(left, piece):
    return jnp.dot(left, piece, preferred_element_type=jnp.float32)


def score_kernel(place_ref, bits_ref, codes_ref, slot_ref, index_ref, out_ref, picks):
    docs = codes_ref.shape[0]
    lanes = picks.shape[1]
    top = index_ref.shape[1]
    entry = lax.broadcasted_iota(jnp.int32, (lanes, docs), 0)
    placing = jnp.where(entry == slot_ref[...], 1.0, 0.0).astype(jnp.bfloat16)
    corpus = jnp.dot(placing, codes_ref[...], preferred_element_type=jnp.float32).astype(
        jnp.bfloat16
    )
    table = lax.dot_general(
        bits_ref[...],
        corpus,
        (((1,), (1,)), ((), ())),
        preferred_element_type=jnp.float32,
    ) * (1.0 / float(bits_ref.shape[1]) ** 0.5)
    picks[...] = jnp.zeros_like(picks)
    picks[:, :top] = index_ref[...]
    out_ref[...] = jnp.take_along_axis(table, picks[...], axis=1)[:, :top]


def score(query_bits, codes, slot_map, query_index, flat_index, rows):
    docs, bits = codes.shape
    top = query_index.shape[1]
    lanes = 128 * max(pl.cdiv(docs, 128), pl.cdiv(top, 128))
    query_index = lax.dynamic_slice_in_dim(query_index, flat_index * rows, rows, 0)
    return pl.pallas_call(
        score_kernel,
        out_shape=jax.ShapeDtypeStruct((rows, top), jnp.float32),
        grid_spec=pltpu.PrefetchScalarGridSpec(
            num_scalar_prefetch=1,
            grid=(1,),
            in_specs=[
                pl.BlockSpec((rows, bits), lambda i, f: (f[0], 0)),
                pl.BlockSpec((docs, bits), lambda i, f: (0, 0)),
                pl.BlockSpec((1, docs), lambda i, f: (0, 0)),
                pl.BlockSpec((rows, top), lambda i, f: (0, 0)),
            ],
            out_specs=pl.BlockSpec((rows, top), lambda i, f: (0, 0)),
            scratch_shapes=[pltpu.VMEM((rows, lanes), jnp.int32)],
        ),
    )(flat_index.reshape(1), query_bits, codes, slot_map[None], query_index)


def wide_kernel(
    states_ref, gain_ref, gate_ref, up_ref, down_ref, out_ref,
    X, G, U, W, AG, AU, H, SR, YR, ZR,
    s_loc, s_y, s_zr, s_zl, s_sib, w_loc, w_x, w_y, w_r, c_sib, c_y, c_z,
):
    nz = lax.axis_size("corpus") // 2
    b = lax.axis_index("batch")
    c = lax.axis_index("corpus")
    y, x = b // 2, b % 2
    z, k = c // 2, c % 2
    rows, feat = states_ref.shape
    half = W.shape[0]
    full = X.shape[1]
    cols = down_ref.shape[1]
    w = cols // 2
    by, bx, bd = (1 - y) * 2 + x, y * 2 + (1 - x), (1 - y) * 2 + (1 - x)
    to_y = {"batch": by}
    to_x = {"batch": bx}
    to_sib = {"corpus": z * 2 + (1 - k)}

    def at_z(other):
        return {"corpus": other * 2 + k}

    def remote(src, dst, sems, place):
        return pltpu.make_async_remote_copy(
            src_ref=src, dst_ref=dst, send_sem=sems.at[0], recv_sem=sems.at[1],
            device_id=place, device_id_type=pl.DeviceIdType.MESH,
        )

    def spot(t, zs, ks):
        block = y if t == 0 else 1 - y
        return X.at[
            pl.ds(pl.multiple_of(block * rows, rows), rows),
            pl.ds(pl.multiple_of((zs * 2 + ks) * feat, feat), feat),
        ]

    own_states = pltpu.make_async_copy(states_ref, spot(0, z, k), s_loc)
    y_states = remote(states_ref, X.at[
        pl.ds(pl.multiple_of(y * rows, rows), rows),
        pl.ds(pl.multiple_of(c * feat, feat), feat),
    ], s_y, to_y)

    def right(t, s):
        src = states_ref if t == 0 and s == 0 else spot(t, z - s, k)
        return remote(src, spot(t, z - s, k), s_zr.at[t, s], at_z(z + 1))

    def left(t, s):
        src = states_ref if t == 0 and s == 0 else spot(t, z + s, k)
        return remote(src, spot(t, z + s, k), s_zl.at[t, s], at_z(z - 1))

    def sib(t, zs):
        return remote(spot(t, zs, k), spot(t, zs, k), s_sib.at[t, zs], to_sib)

    def sib_in(t, zs):
        return remote(spot(t, zs, 1 - k), spot(t, zs, 1 - k), s_sib.at[t, zs], to_sib)

    def first(t):
        @pl.when(z + 1 < nz)
        def _():
            right(t, 0).start()

        @pl.when(z >= 1)
        def _():
            left(t, 0).start()

        sib(t, z).start()

    def relay(t, s):
        @pl.when(z - 1 - s >= 0)
        def _():
            right(t, s).wait_recv()
            if s + 1 < nz - 1:
                @pl.when(z + 1 < nz)
                def _():
                    right(t, s + 1).start()
            sib(t, z - 1 - s).start()

        @pl.when(z + 1 + s < nz)
        def _():
            left(t, s).wait_recv()
            if s + 1 < nz - 1:
                @pl.when(z >= 1)
                def _():
                    left(t, s + 1).start()
            sib(t, z + 1 + s).start()

    def part(m, mine):
        h = pl.ds(pl.multiple_of((y if mine else 1 - y) * half, half), half)
        if m == 2:
            return down_ref.at[h, :]
        return (gate_ref, up_ref)[m].at[:, h]

    def place(m, block):
        if m == 2:
            return W.at[:, pl.ds(pl.multiple_of(block * cols, cols), cols)]
        return (G, U)[m].at[pl.ds(pl.multiple_of(block * rows_w, rows_w), rows_w), :]

    rows_w = gate_ref.shape[0]
    loc = [pltpu.make_async_copy(part(m, True), place(m, b), w_loc.at[m]) for m in range(3)]
    wx = [remote(part(m, True), place(m, b), w_x.at[m], to_x) for m in range(3)]
    wy = [remote(part(m, False), place(m, b), w_y.at[m], to_y) for m in range(3)]
    wr = [remote(place(m, by), place(m, by), w_r.at[m], to_x) for m in range(3)]

    def settle(t):
        for zs in range(nz):
            sib_in(t, zs).wait_recv()
            sib(t, zs).wait_send()
        for s in range(nz - 1):
            @pl.when((z - s >= 0) & (z + 1 < nz))
            def _():
                right(t, s).wait_send()

            @pl.when((z + s < nz) & (z >= 1))
            def _():
                left(t, s).wait_send()

    gain = gain_ref[...]
    strip = min(512, rows)
    tile = min(256, rows)
    step = half // 3 if half % 384 == 0 else 128
    blocks = [x, 2 + x, 1 - x, 2 + (1 - x)]
    own_rows = out_ref.shape[0]

    def norm(t):
        start = (y if t == 0 else 1 - y) * rows

        @pl.loop(0, rows // 32)
        def _(p):
            r = pl.ds(pl.multiple_of(start + p * 32, 32), 32)
            v = X[r, :].astype(jnp.float32)
            scale = lax.rsqrt(jnp.mean(v * v, axis=-1, keepdims=True) + 1e-06)
            X[r, :] = (v * scale * gain).astype(jnp.bfloat16)

    def block_product(block, order):
        depth = pl.ds(pl.multiple_of(block * rows_w, rows_w), rows_w)

        @pl.loop(0, rows // strip)
        def _(i):
            here = pl.ds(pl.multiple_of(i * strip, strip), strip)
            r = pl.ds(pl.multiple_of((1 - y) * rows + i * strip, strip), strip)

            @pl.loop(0, half // step)
            def _(j):
                h = pl.ds(pl.multiple_of(j * step, 128), step)
                g = jnp.dot(X[r, depth], G[depth, h], preferred_element_type=jnp.float32)
                u = jnp.dot(X[r, depth], U[depth, h], preferred_element_type=jnp.float32)
                if order > 0:
                    g = g + AG[here, h]
                    u = u + AU[here, h]
                if order < 3:
                    AG[here, h] = g
                    AU[here, h] = u
                else:
                    H[r, h] = (g * jax.nn.sigmoid(g) * u).astype(jnp.bfloat16)

    def own_product(low, high):
        @pl.loop(low, high)
        def _(i):
            r = pl.ds(pl.multiple_of(y * rows + i * tile, tile), tile)

            @pl.loop(0, half // step)
            def _(j):
                h = pl.ds(pl.multiple_of(j * step, 128), step)
                g = jnp.dot(X[r, :], G[:, h], preferred_element_type=jnp.float32)
                u = jnp.dot(X[r, :], U[:, h], preferred_element_type=jnp.float32)
                H[r, h] = (g * jax.nn.sigmoid(g) * u).astype(jnp.bfloat16)

    y_states.start()
    own_states.start()
    wx[0].start()
    for m in range(3):
        wy[m].start()
    wx[1].start()
    own_states.wait()
    first(0)
    for m in range(3):
        loc[m].start()
    y_states.wait_recv()
    first(1)
    for s in range(nz - 1):
        relay(1, s)
        if s == 0:
            wy[0].wait_recv()
            wr[0].start()
    wy[1].wait_recv()
    wr[1].start()
    relay(0, 0)
    settle(1)
    norm(1)
    for s in range(1, nz - 1):
        if s == nz - 2:
            for m in range(2):
                loc[m].wait()
            block_product(b, 0)
            block_product(by, 1)
            for m in range(2):
                wx[m].wait_recv()
            block_product(bx, 2)
            wy[2].wait_recv()

            @pl.when(y == 0)
            def _():
                wx[2].start()
                wr[2].start()

            @pl.when(y == 1)
            def _():
                wr[2].start()
                wx[2].start()

        relay(0, s)
    settle(0)
    for j in range(4):
        out_ref[:, pl.ds(pl.multiple_of(blocks[j] * w, w), w)] = X[
            pl.ds(pl.multiple_of(y * rows + z * own_rows, own_rows), own_rows),
            pl.ds(pl.multiple_of(blocks[j] * cols + k * w, w), w),
        ].astype(jnp.float32)
    norm(0)
    for m in range(2):
        wr[m].wait_recv()
    block_product(bd, 3)
    loc[2].wait()

    base = full // 2

    def down_cols(j, core):
        return pl.ds(pl.multiple_of(blocks[j] * cols + core * w, w), w)

    def block_rows(t):
        return pl.ds(pl.multiple_of((y if t == 0 else 1 - y) * rows, rows), rows)

    def sib_sum(t, j):
        return remote(
            X.at[block_rows(t), pl.ds(j * w, w)], SR.at[j, block_rows(t), :],
            c_sib.at[t, j], to_sib,
        )

    hw = w // 2

    def y_sum(j, h):
        return remote(
            X.at[block_rows(1), pl.ds(base + j * w + h * hw, hw)],
            YR.at[j, :, pl.ds(h * hw, hw)], c_y.at[j, h], to_y,
        )

    def z_sum(j, h, dz):
        to = lax.rem(z + dz, nz)
        return remote(
            X.at[
                pl.ds(pl.multiple_of(y * rows + to * own_rows, own_rows), own_rows),
                pl.ds(base + j * w + h * hw, hw),
            ],
            ZR.at[j, dz - 1, :, pl.ds(h * hw, hw)], c_z.at[j, h, dz - 1], at_z(to),
        )

    def strips(t):
        start = (y if t == 0 else 1 - y) * rows
        return lambda i: pl.ds(pl.multiple_of(start + i * strip, strip), strip)

    def step_a(t, j):
        @pl.loop(0, rows // strip)
        def _(i):
            r = strips(t)(i)
            X[r, pl.ds(j * w, w)] = jnp.dot(
                H[r, :], W[:, down_cols(j, 1 - k)], preferred_element_type=jnp.float32
            ).astype(jnp.bfloat16)

        sib_sum(t, j).start()

    def step_b(t, j):
        sib_sum(t, j).wait_recv()
        for h in range(2):
            down = pl.ds(pl.multiple_of(blocks[j] * cols + k * w + h * hw, hw), hw)

            @pl.loop(0, rows // strip)
            def _(i):
                r = strips(t)(i)
                X[r, pl.ds(base + j * w + h * hw, hw)] = (
                    jnp.dot(H[r, :], W[:, down], preferred_element_type=jnp.float32)
                    + SR[j, r, pl.ds(h * hw, hw)].astype(jnp.float32)
                ).astype(jnp.bfloat16)

            if t == 1:
                y_sum(j, h).start()

    def half_c(j, h):
        y_sum(j, h).wait_recv()

        @pl.loop(0, rows // own_rows)
        def _(i):
            r = pl.ds(pl.multiple_of(y * rows + i * own_rows, own_rows), own_rows)
            here = pl.ds(base + j * w + h * hw, hw)
            q = pl.ds(pl.multiple_of(i * own_rows, own_rows), own_rows)
            X[r, here] = (
                X[r, here].astype(jnp.float32)
                + YR[j, q, pl.ds(h * hw, hw)].astype(jnp.float32)
            ).astype(jnp.bfloat16)

        for dz in range(1, nz):
            z_sum(j, h, dz).start()

    def step_c(j):
        half_c(j, 0)
        half_c(j, 1)

    def half_e(j, h):
        here = pl.ds(pl.multiple_of(blocks[j] * w + h * hw, hw), hw)
        total = out_ref[:, here] + X[
            pl.ds(pl.multiple_of(y * rows + z * own_rows, own_rows), own_rows),
            pl.ds(base + j * w + h * hw, hw),
        ].astype(jnp.float32)
        for dz in range(1, nz):
            z_sum(j, h, dz).wait_recv()
            total = total + ZR[j, dz - 1, :, pl.ds(h * hw, hw)].astype(jnp.float32)
        out_ref[:, here] = total

    def step_e(j):
        half_e(j, 0)
        half_e(j, 1)

    def down_from_x(low):
        @pl.when(y == (0 if low else 1))
        def _():
            wx[2].wait_recv()

        @pl.when(y == (1 if low else 0))
        def _():
            wr[2].wait_recv()

    tiles = rows // tile
    step_a(1, 0)
    step_a(1, 1)
    own_product(0, 1)
    step_b(1, 0)
    step_b(1, 1)
    own_product(1, tiles)
    step_a(0, 0)
    step_a(0, 1)
    down_from_x(True)
    step_a(1, 2)
    step_a(0, 2)
    step_b(0, 0)
    step_b(1, 2)
    step_c(0)
    step_b(0, 1)
    step_b(0, 2)
    step_c(1)
    down_from_x(False)
    step_a(1, 3)
    step_a(0, 3)
    step_b(1, 3)
    step_b(0, 3)
    step_e(0)
    step_c(2)
    half_c(3, 0)
    step_e(1)
    half_c(3, 1)
    step_e(2)
    step_e(3)
    for j in range(4):
        sib_sum(0, j).wait_send()
        sib_sum(1, j).wait_send()
        for h in range(2):
            y_sum(j, h).wait_send()
            for dz in range(1, nz):
                z_sum(j, h, dz).wait_send()
    y_states.wait_send()
    for m in range(3):
        wx[m].wait_send()
        wy[m].wait_send()
        wr[m].wait_send()


def wide(states, norm_gain, gate_weight, up_weight, down_weight):
    nz = lax.axis_size("corpus") // 2
    rows, feat = states.shape
    full = norm_gain.shape[0]
    half = gate_weight.shape[1] // 2
    cols = down_weight.shape[1]
    w = cols // 2
    own_rows = rows // nz
    dma = pltpu.SemaphoreType.DMA
    any_spec = pl.BlockSpec(memory_space=pl.ANY)
    vmem = pl.BlockSpec(memory_space=pltpu.VMEM)
    return pl.pallas_call(
        wide_kernel,
        out_shape=jax.ShapeDtypeStruct((own_rows, full // 2), jnp.float32),
        in_specs=[any_spec, vmem, any_spec, any_spec, any_spec],
        out_specs=vmem,
        scratch_shapes=[
            pltpu.VMEM((2 * rows, full), jnp.bfloat16),
            pltpu.VMEM((full, half), jnp.bfloat16),
            pltpu.VMEM((full, half), jnp.bfloat16),
            pltpu.VMEM((half, full), jnp.bfloat16),
            pltpu.VMEM((rows, half), jnp.float32),
            pltpu.VMEM((rows, half), jnp.float32),
            pltpu.VMEM((2 * rows, half), jnp.bfloat16),
            pltpu.VMEM((4, 2 * rows, w), jnp.bfloat16),
            pltpu.VMEM((4, rows, w), jnp.bfloat16),
            pltpu.VMEM((4, nz - 1, own_rows, w), jnp.bfloat16),
            dma, dma((2,)), dma((2, nz - 1, 2)), dma((2, nz - 1, 2)), dma((2, nz, 2)),
            dma((3,)), dma((3, 2)), dma((3, 2)), dma((3, 2)),
            dma((2, 4, 2)), dma((4, 2, 2)), dma((4, 2, nz - 1, 2)),
        ],
        compiler_params=pltpu.CompilerParams(
            has_side_effects=True, vmem_limit_bytes=67043328
        ),
    )(states, norm_gain[None], gate_weight, up_weight, down_weight)


def code_kernel(resid_ref, gain_ref, hash_ref, out_ref, HV, SQ, PB, CA, h_sem, q_sem, p_sem, a_send, a_recv):
    corpus = lax.axis_size("corpus")
    devices = lax.axis_size("batch") * corpus
    b = lax.axis_index("batch")
    c = lax.axis_index("corpus")
    k = c % 2
    me = b * corpus + c
    to_sib = {"corpus": c + 1 - 2 * k}
    own_rows, full_half = resid_ref.shape
    w = HV.shape[1]
    docs = own_rows // DOC_LEN
    fetch = pltpu.make_async_copy(
        hash_ref.at[:, pl.ds(pl.multiple_of(k * w, w), w)], HV, h_sem
    )
    fetch.start()

    def swap(buf, sems):
        return pltpu.make_async_remote_copy(
            src_ref=buf.at[0], dst_ref=buf.at[1], send_sem=sems.at[0], recv_sem=sems.at[1],
            device_id=to_sib, device_id_type=pl.DeviceIdType.MESH,
        )

    square = jnp.sum(resid_ref[...] * resid_ref[...], axis=1, keepdims=True)
    SQ[0] = jnp.broadcast_to(square, SQ.shape[1:])
    swap(SQ, q_sem).start()
    swap(SQ, q_sem).wait()
    scale = lax.rsqrt((square + SQ[1][:, :1]) / float(2 * full_half) + 1e-06)
    final = resid_ref[...] * scale * gain_ref[...]
    pooled = [
        jnp.mean(final[d * DOC_LEN : (d + 1) * DOC_LEN], axis=0, keepdims=True)
        for d in range(docs)
    ]
    pooled.append(jnp.zeros((PB.shape[1] - docs, full_half), jnp.float32))
    PB[0] = jnp.concatenate(pooled, axis=0).astype(jnp.bfloat16)
    swap(PB, p_sem).start()
    fetch.wait()
    swap(PB, p_sem).wait()
    total = None
    parts = lax.axis_size("batch")
    span = full_half // parts
    for n in range(parts):
        for side in range(2):
            core = k if side == 0 else 1 - k
            term = jnp.dot(
                PB[side, :, n * span : (n + 1) * span],
                HV[pl.ds(pl.multiple_of(n * 2 * span + core * span, span), span), :],
                preferred_element_type=jnp.float32,
            )
            total = term if total is None else total + term
    codes = jnp.tanh(total)[:docs]
    lanes = CA.shape[2]
    CA[me] = jnp.concatenate(
        [codes[:, q * lanes : (q + 1) * lanes] for q in range(w // lanes)], axis=0
    ).astype(jnp.bfloat16)

    def tell(step):
        to = lax.rem(me + step, devices)
        return pltpu.make_async_remote_copy(
            src_ref=CA.at[me], dst_ref=CA.at[me],
            send_sem=a_send.at[step - 1], recv_sem=a_recv.at[step - 1],
            device_id={"batch": to // corpus, "corpus": to % corpus},
            device_id_type=pl.DeviceIdType.MESH,
        )

    def heard(step):
        src = lax.rem(me + devices - step, devices)
        return pltpu.make_async_remote_copy(
            src_ref=CA.at[src], dst_ref=CA.at[src],
            send_sem=a_send.at[step - 1], recv_sem=a_recv.at[step - 1],
            device_id={"batch": src // corpus, "corpus": src % corpus},
            device_id_type=pl.DeviceIdType.MESH,
        )

    @pl.loop(1, devices)
    def _(step):
        tell(step).start()

    @pl.loop(1, devices)
    def _(step):
        heard(step).wait_recv()

    @pl.loop(1, devices)
    def _(step):
        tell(step).wait_send()

    out_ref[...] = CA[...]


def all_codes(resid, final_gain, hash_weight):
    parts = lax.axis_size("batch")
    corpus = lax.axis_size("corpus")
    devices = parts * corpus
    own_rows, full_half = resid.shape
    docs = own_rows // DOC_LEN
    bits = hash_weight.shape[1]
    w = bits // 2
    gain = lax.dynamic_index_in_dim(
        final_gain.reshape(parts, 2, full_half // parts), lax.axis_index("corpus") % 2, 1, False
    ).reshape(1, full_half)
    vmem = pl.BlockSpec(memory_space=pltpu.VMEM)
    dma = pltpu.SemaphoreType.DMA
    groups = w // 128
    got = pl.pallas_call(
        code_kernel,
        out_shape=jax.ShapeDtypeStruct((devices, groups * docs, 128), jnp.bfloat16),
        in_specs=[vmem, vmem, pl.BlockSpec(memory_space=pl.ANY)],
        out_specs=vmem,
        scratch_shapes=[
            pltpu.VMEM((2 * full_half, w), jnp.bfloat16),
            pltpu.VMEM((2, own_rows, 128), jnp.float32),
            pltpu.VMEM((2, 16, full_half), jnp.bfloat16),
            pltpu.VMEM((devices, groups * docs, 128), jnp.bfloat16),
            dma, dma((2,)), dma((2,)), dma((devices - 1,)), dma((devices - 1,)),
        ],
        compiler_params=pltpu.CompilerParams(
            has_side_effects=True, vmem_limit_bytes=67043328
        ),
    )(resid, gain, hash_weight)
    got = got.reshape(parts, corpus // 2, 2, groups, docs, 128)
    return got.transpose(0, 1, 4, 2, 3, 5).reshape(devices // 2 * docs, bits)


def plain_codes(
    states, norm_gain, gate_weight, up_weight, down_weight, final_gain, hash_weight
):
    whole = lax.all_gather(states, "corpus", axis=1, tiled=True)
    normed = rms(whole.astype(jnp.float32), norm_gain).astype(jnp.bfloat16)

    def add_one(piece):
        return add_rows(normed, piece)

    gate = add_one(lax.all_gather(gate_weight, "batch", axis=0, tiled=True))
    up = add_one(lax.all_gather(up_weight, "batch", axis=0, tiled=True))
    hidden = (jax.nn.silu(gate) * up).astype(jnp.bfloat16)
    terms = jnp.dot(
        hidden,
        lax.all_gather(down_weight, "batch", axis=1, tiled=True),
        preferred_element_type=jnp.float32,
    )
    ffn = lax.psum_scatter(
        terms.astype(jnp.bfloat16), "corpus", scatter_dimension=0, tiled=True
    ).astype(jnp.float32)
    own_rows = ffn.shape[0]
    mine = lax.dynamic_slice_in_dim(whole, lax.axis_index("corpus") * own_rows, own_rows, 0)
    resid = mine.astype(jnp.float32) + ffn
    finals = rms(resid, final_gain)
    owned_docs = own_rows // DOC_LEN
    pooled = jnp.mean(finals.reshape(owned_docs, DOC_LEN, finals.shape[1]), axis=1).astype(
        jnp.bfloat16
    )
    codes = jnp.tanh(jnp.dot(pooled, hash_weight, preferred_element_type=jnp.float32)).astype(
        jnp.bfloat16
    )
    return lax.all_gather(codes, ("batch", "corpus"), axis=0, tiled=True)


def local(
    states,
    norm_gain,
    gate_weight,
    up_weight,
    down_weight,
    final_gain,
    hash_weight,
    query_bits,
    slot_map,
    query_index,
):
    corpus_count = lax.axis_size("corpus")
    devices = lax.axis_size("batch") * corpus_count
    flat_index = lax.axis_index("batch") * corpus_count + lax.axis_index("corpus")
    layer = (states, norm_gain, gate_weight, up_weight, down_weight)
    if lax.axis_size("batch") == 4 and corpus_count == 8:
        gathered = all_codes(wide(*layer), final_gain, hash_weight)
    else:
        gathered = plain_codes(*layer, final_gain, hash_weight)
    query_rows = query_bits.shape[0] // devices
    return score(query_bits, gathered, slot_map, query_index, flat_index, query_rows)


def solution(mesh):
    placed = (
        P("batch", "corpus"),
        P(),
        P("batch", "corpus"),
        P("batch", "corpus"),
        P("corpus", "batch"),
        P(),
        P(),
        P(),
        P(),
        P(),
    )
    return jax.shard_map(
        local, mesh=mesh, in_specs=placed, out_specs=P(("batch", "corpus"), None), check_vma=False
    )
```
